1024 devices in a mesh: face: 16 (over z), blk: 64 (over y, x, core).
Axes of the slice: x: 4, y: 8, z: 16, core: 2. Of those that a mesh axis runs over, the one named last changes fastest.
Arguments:
- air_state: float32 [3, 16, 256, 8192], P(None, None, 'face', 'blk'), may hold values from -6 to 6
- air_wind: float32 [2, 16, 256, 8192], P(None, None, 'face', 'blk'), may hold values from -4 to 4
- jacobian: float32 [256, 8192], P('face', 'blk'), may hold values from 0.5 to 2
- land_area: float32 [256, 8192], P('face', 'blk'), may hold values from 0.1 to 1
- xgrid_rows: int32 [1024, 64, 128], P(('face', 'blk')), may hold values from 0 to 2047
- tracers: float32 [2, 16, 2097152], P(None, None, ('face', 'blk')), may hold values from -6 to 6
- edge_coef: float32 [6, 2097152], P(None, ('face', 'blk')), may hold values from 0.02 to 0.14
- neighbours: int32 [6, 2097152], P(None, ('face', 'blk')), may hold values from 0 to 2303
- vert_rate: float32 [2097152], P(('face', 'blk')), may hold values from 0.05 to 0.2
- ocean_area: float32 [2097152], P(('face', 'blk')), may hold values from 0.5 to 2
- send_list: int32 [1024, 256], P(('face', 'blk')), may hold values from 0 to 2047
- xgrid_cols: int32 [1024, 64, 128], P(('face', 'blk')), may hold values from 0 to 2047
- xgrid_weights: float32 [1024, 64, 128], P(('face', 'blk')), may hold values from 0 to 1, as said below
Outputs:
- air_final: float32 [3, 16, 256, 8192], P(None, None, 'face', 'blk')
- ocean_final: float32 [2, 16, 2097152], P(None, None, ('face', 'blk'))
The draws below stay inside these ranges and needn't reach their ends.
Inputs may be any that keep to these rules, and one draw needn't show every extreme that they name: `xgrid_weights`: in every block of 128 slots the nonzero weights, each at least 0.1, come first and zeros fill the rest; in every draw some blocks of every device are completely full.
All inputs are finite; a program needn't handle non-finite values.
Results may differ from the reference program's by a relative error of at most 0.00016.
Values sent between devices are 32-bit elements; how exact they have to be, the bound alone decides.
A program may use at most 64 MiB of HBM per device.

```python
import math
import jax
import jax.numpy as jnp
from jax import lax

GLL = 4
FIELDS = 3
LEVELS = 16
SUBSTEPS = 2
OCN_TRACERS = 2
OCEAN_LEVELS = 16
EDGES = 6
CELLS_DEV = 2048
RIM = 128
SLOTS = 128
PX = 16
PY = 128
GX = 256
GY = 8192
CELLS = 2097152
N_FACE = 16
N_BLK = 64
DEVICES = 1024


def draw_xgrid_weights(key, part):
    base = jax.random.fold_in(key, 7301)
    key_count, key_busy, key_full, key_value = jax.random.split(base, 4)
    counts = jax.random.randint(key_count, (DEVICES, N_BLK), 0, SLOTS + 1)
    busy = jax.random.randint(key_busy, (DEVICES, 1), 0, 4) == 0
    counts = jnp.where(busy, SLOTS, counts)
    full_peer = jax.random.randint(key_full, (DEVICES, 1), 0, N_BLK)
    counts = jnp.where(jnp.arange(N_BLK)[None, :] == full_peer, SLOTS, counts)
    live = jnp.arange(SLOTS)[None, None, :] < counts[:, :, None]
    values = jnp.exp(jax.random.uniform(key_value, (DEVICES, N_BLK, SLOTS), jnp.float32, jnp.log(0.1), 0.0))
    return jnp.where(live, values, 0.0).astype(jnp.float32)


def with_ends(entries, stream_key, low, top_value):
    index_at = [jax.random.randint(jax.random.fold_in(stream_key, axis), (), 0, length) for axis, length in enumerate(entries.shape)]
    longest = entries.shape.index(max(entries.shape))
    next_to = index_at[:longest] + [(index_at[longest] + 1) % entries.shape[longest]] + index_at[longest + 1:]
    return entries.at[tuple(index_at)].set(low).at[tuple(next_to)].set(top_value)


def shard_levels(rng, extent, shards, smallest, high):
    level = 1.0
    for position, blocks in shards:
        heights = jax.random.uniform(jax.random.fold_in(jax.random.fold_in(rng, 6), position), (blocks,), jnp.float32, smallest / len(shards), high / len(shards))
        level = level * jnp.repeat(jnp.exp(heights), extent[position] // blocks).reshape((-1,) + (1,) * (len(extent) - 1 - position))
    return level


def noise(rng, extent, width, limit, cuts=(), kind=jnp.bfloat16):
    drawn = width * jax.random.normal(rng, extent, jnp.float32)
    if cuts:
        drawn = drawn * shard_levels(rng, extent, cuts, -0.22, 0.18)
    return jnp.clip(drawn, -limit, limit).astype(kind)


def setup_inputs(seed: int = 0) -> dict:
    seeds = jax.random.split(jax.random.key(seed), 14)
    air_state = noise(seeds[0], (FIELDS, LEVELS, GX, GY), 1.0, 6.0, ((2, 16), (3, 64)), jnp.float32)
    air_wind = noise(seeds[1], (2, LEVELS, GX, GY), 1.0, 4.0, ((2, 16), (3, 64)), jnp.float32)
    jacobian = jnp.clip(jnp.exp(math.log(2.0) - 1.3862944 * jax.random.uniform(seeds[2], (GX, GY), jnp.float32) ** shard_levels(seeds[2], (GX, GY), ((0, 16), (1, 64)), -0.2, 0.2)), 0.5, 2.0)
    land_area = jnp.clip(jnp.exp(math.log(1.0) - 2.3025851 * jax.random.uniform(seeds[3], (GX, GY), jnp.float32) ** shard_levels(seeds[3], (GX, GY), ((0, 16), (1, 64)), -0.2, 0.2)), 0.1, 1.0)
    xgrid_rows = with_ends(jax.random.randint(seeds[4], (N_FACE * N_BLK, N_BLK, SLOTS), 0, PX * PY), jax.random.fold_in(seeds[4], 1), 0, (PX * PY) - 1).astype(jnp.int32)
    tracers = noise(seeds[5], (OCN_TRACERS, OCEAN_LEVELS, CELLS), 1.0, 6.0, ((2, 1024),), jnp.float32)
    edge_coef = jnp.clip(jnp.exp(math.log(0.14) - 1.9459102 * jax.random.uniform(seeds[6], (EDGES, CELLS), jnp.float32) ** shard_levels(seeds[6], (EDGES, CELLS), ((1, 1024),), -0.2, 0.2)), 0.02, 0.14)
    neighbours = with_ends(jax.random.randint(seeds[7], (EDGES, CELLS), 0, CELLS_DEV + 2 * RIM), jax.random.fold_in(seeds[7], 1), 0, (CELLS_DEV + 2 * RIM) - 1).astype(jnp.int32)
    vert_rate = jnp.clip(jnp.exp(math.log(0.2) - 1.3862944 * jax.random.uniform(seeds[8], (CELLS,), jnp.float32) ** shard_levels(seeds[8], (CELLS,), ((0, 1024),), -0.2, 0.2)), 0.05, 0.2)
    ocean_area = jnp.clip(jnp.exp(math.log(2.0) - 1.3862944 * jax.random.uniform(seeds[9], (CELLS,), jnp.float32) ** shard_levels(seeds[9], (CELLS,), ((0, 1024),), -0.2, 0.2)), 0.5, 2.0)
    send_list = with_ends(jax.random.randint(seeds[10], (N_FACE * N_BLK, 2 * RIM), 0, CELLS_DEV), jax.random.fold_in(seeds[10], 1), 0, CELLS_DEV - 1).astype(jnp.int32)
    xgrid_cols = with_ends(jax.random.randint(seeds[11], (N_FACE * N_BLK, N_BLK, SLOTS), 0, CELLS_DEV), jax.random.fold_in(seeds[11], 1), 0, CELLS_DEV - 1).astype(jnp.int32)
    xgrid_weights = draw_xgrid_weights(jax.random.fold_in(seeds[13], 71), 0)
    return dict(air_state=air_state, air_wind=air_wind, jacobian=jacobian, land_area=land_area, xgrid_rows=xgrid_rows, tracers=tracers, edge_coef=edge_coef, neighbours=neighbours, vert_rate=vert_rate, ocean_area=ocean_area, send_list=send_list, xgrid_cols=xgrid_cols, xgrid_weights=xgrid_weights)


deriv_table = [[-3.0, 4.045084971874737, -1.545084971874737, 0.5], [-0.8090169943749475, 0.0, 1.118033988749895, -0.30901699437494745], [0.30901699437494745, -1.118033988749895, 0.0, 0.8090169943749475], [-0.5, 1.545084971874737, -4.045084971874737, 3.0]]
gll_weights = [1.0 / 6.0, 5.0 / 6.0, 5.0 / 6.0, 1.0 / 6.0]
time_step = 0.05
relax_rate = 0.3
flux_gain = 0.2


def along_first(field):
    table = jnp.array(deriv_table, jnp.float32)
    planes, xsize, ysize = field.shape
    shaped = field.reshape(planes, xsize // GLL, GLL, ysize)
    result = jnp.einsum("ik,aeky->aeiy", table, shaped, precision=lax.Precision.HIGHEST)
    return result.reshape(planes, xsize, ysize)


def along_second(field):
    table = jnp.array(deriv_table, jnp.float32)
    planes, xsize, ysize = field.shape
    shaped = field.reshape(planes, xsize, ysize // GLL, GLL)
    result = jnp.einsum("ik,axek->axei", table, shaped, precision=lax.Precision.HIGHEST)
    return result.reshape(planes, xsize, ysize)


def copy_sum(values):
    xsize, ysize = values.shape[-2], values.shape[-1]
    x_pos = jnp.arange(xsize, dtype=jnp.int32) % GLL
    y_pos = jnp.arange(ysize, dtype=jnp.int32) % GLL
    first_row = (x_pos == 0)[:, None]
    last_row = (x_pos == GLL - 1)[:, None]
    partial_sum = values + jnp.where(first_row, jnp.roll(values, 1, -2), 0.0) + jnp.where(last_row, jnp.roll(values, -1, -2), 0.0)
    first_col = y_pos == 0
    last_col = y_pos == GLL - 1
    return partial_sum + jnp.where(first_col, jnp.roll(partial_sum, 1, -1), 0.0) + jnp.where(last_col, jnp.roll(partial_sum, -1, -1), 0.0)


def reference(air_state, air_wind, jacobian, land_area, xgrid_rows, tracers, edge_coef, neighbours, vert_rate, ocean_area, send_list, xgrid_cols, xgrid_weights):
    field_count, levels, gx_all, gy_all = air_state.shape
    x_points = gx_all // N_FACE
    y_points = gy_all // N_BLK
    block_points = x_points * y_points
    ocn_count, ocn_levels, cell_total = tracers.shape
    cell_count = cell_total // (N_FACE * N_BLK)
    slot_count = xgrid_rows.shape[2]
    rim_width = send_list.shape[1] // 2

    def to_blocks(grid):
        return grid.reshape(N_FACE, x_points, N_BLK, y_points).transpose(0, 2, 1, 3).reshape(N_FACE, N_BLK, block_points)

    def from_blocks(flat):
        return flat.reshape(N_FACE, N_BLK, x_points, y_points).transpose(0, 2, 1, 3).reshape(gx_all, gy_all)

    point_ids = xgrid_rows.reshape(N_FACE, N_BLK, N_BLK, slot_count)
    cell_ids = xgrid_cols.reshape(N_FACE, N_BLK, N_BLK, slot_count)
    weights = xgrid_weights.reshape(N_FACE, N_BLK, N_BLK, slot_count)

    surface = tracers[0, 0].reshape(N_FACE, N_BLK, cell_count)
    surface_at = jnp.take_along_axis(surface, cell_ids.reshape(N_FACE, N_BLK, N_BLK * slot_count), axis=2).reshape(N_FACE, N_BLK, N_BLK, slot_count)
    heat_terms = (weights * surface_at).transpose(0, 2, 1, 3)
    frac_terms = weights.transpose(0, 2, 1, 3)
    point_base = (jnp.arange(N_FACE * N_BLK, dtype=jnp.int32) * block_points).reshape(N_FACE, N_BLK, 1, 1)
    point_targets = (point_base + point_ids).reshape(-1).astype(jnp.int32)
    heat_sum = jax.ops.segment_sum(heat_terms.reshape(-1), point_targets, num_segments=N_FACE * N_BLK * block_points)
    frac_sum = jax.ops.segment_sum(frac_terms.reshape(-1), point_targets, num_segments=N_FACE * N_BLK * block_points)
    heat_map = from_blocks(heat_sum)
    frac_map = from_blocks(frac_sum)
    t_surf = (heat_map + land_area * air_state[0, 0]) / (frac_map + land_area)

    table = jnp.array(gll_weights, jnp.float32)
    x_weight = table[jnp.arange(gx_all, dtype=jnp.int32) % GLL]
    y_weight = table[jnp.arange(gy_all, dtype=jnp.int32) % GLL]
    mass_map = x_weight[:, None] * y_weight[None, :] * jacobian
    mass_sum = copy_sum(mass_map)

    def advance(packed):
        field, flag = packed
        for substep in range(SUBSTEPS):
            tendency = -(air_wind[0] * along_first(field) + air_wind[1] * along_second(field))
            moved = field + time_step * tendency
            moved = moved.at[0].add(flag * relax_rate * (t_surf - field[0]))
            field = copy_sum(mass_map * moved) / mass_sum
        return field

    flags = (jnp.arange(field_count, dtype=jnp.int32) == 0).astype(jnp.float32)
    air_final = lax.map(advance, (air_state, flags))

    sea_flux = to_blocks(air_final[0, 0] - t_surf)
    sent = jnp.take_along_axis(sea_flux, point_ids.reshape(N_FACE, N_BLK, N_BLK * slot_count), axis=2).reshape(N_FACE, N_BLK, N_BLK, slot_count)
    arrived = sent.transpose(0, 2, 1, 3)
    cell_base = (jnp.arange(N_FACE * N_BLK, dtype=jnp.int32) * cell_count).reshape(N_FACE, N_BLK, 1, 1)
    cell_targets = (cell_base + cell_ids).reshape(-1).astype(jnp.int32)
    inflow = jax.ops.segment_sum((weights * arrived).reshape(-1), cell_targets, num_segments=N_FACE * N_BLK * cell_count)

    tracer_blocks = tracers.reshape(ocn_count, ocn_levels, N_FACE, N_BLK, cell_count)
    send_ids = send_list.reshape(N_FACE, N_BLK, 2 * rim_width)
    send_full = jnp.broadcast_to(send_ids[None, None], (ocn_count, ocn_levels, N_FACE, N_BLK, 2 * rim_width))
    outgoing = jnp.take_along_axis(tracer_blocks, send_full, axis=4)
    lower_rim = jnp.roll(outgoing[..., rim_width:], 1, axis=3)
    upper_rim = jnp.roll(outgoing[..., :rim_width], -1, axis=3)
    extended = jnp.concatenate([tracer_blocks, lower_rim, upper_rim], axis=4)
    near_ids = neighbours.reshape(EDGES, N_FACE, N_BLK, cell_count)
    coef_blocks = edge_coef.reshape(EDGES, N_FACE, N_BLK, cell_count)
    lateral = jnp.zeros_like(tracer_blocks)
    for edge in range(EDGES):
        index_full = jnp.broadcast_to(near_ids[edge][None, None], tracer_blocks.shape)
        adjacent = jnp.take_along_axis(extended, index_full, axis=4)
        lateral = lateral + coef_blocks[edge] * (adjacent - tracer_blocks)
    lateral = lateral.reshape(ocn_count, ocn_levels, cell_total)
    upper_level = jnp.concatenate([tracers[:, :1], tracers[:, :-1]], axis=1)
    lower_level = jnp.concatenate([tracers[:, 1:], tracers[:, -1:]], axis=1)
    vertical = vert_rate * ((upper_level - tracers) + (lower_level - tracers))
    ocean_final = tracers + lateral + vertical
    ocean_final = ocean_final.at[0, 0].add(flux_gain * inflow / ocean_area)
    return air_final, ocean_final
```

```python
import jax
import jax.numpy as jnp
import numpy as np
from jax import lax
from jax.experimental import pallas as pl
from jax.experimental.pallas import tpu as pltpu
from jax.sharding import Mesh
from jax.sharding import PartitionSpec as P

GLL = 4
SUBSTEPS = 2
BLK = ("blk_0", "blk_1", "blk_2")
FACE_BLK = ("face", "blk_0", "blk_1", "blk_2")


deriv_table = [
    [-3.0, 4.045084971874737, -1.545084971874737, 0.5],
    [-0.8090169943749475, 0.0, 1.118033988749895, -0.30901699437494745],
    [0.30901699437494745, -1.118033988749895, 0.0, 0.8090169943749475],
    [-0.5, 1.545084971874737, -4.045084971874737, 3.0],
]
time_step = 0.05
relax_rate = 0.3
flux_gain = 0.2


def with_halo(block, sides, width):
    for axis, dim in sides:
        count = lax.axis_size(axis)
        forward = [(i, i + 1) for i in range(count - 1)]
        forward.append((count - 1, 0))
        backward = [(target, source) for source, target in forward]
        low = lax.ppermute(
            lax.slice_in_dim(block, block.shape[dim] - width, None, axis=dim), axis, forward
        )
        high = lax.ppermute(lax.slice_in_dim(block, 0, width, axis=dim), axis, backward)
        block = jnp.concatenate([low, block, high], axis=dim)
    return block


def split_up(value, dim, peers):
    before, after = (value.shape[:dim], value.shape[dim + 1 :])
    return jnp.moveaxis(value.reshape(*before, peers, -1, *after), dim, 0)


def joined_along(parts, dim):
    shape = list(parts.shape[1:])
    shape[dim] *= parts.shape[0]
    return jnp.moveaxis(parts, 0, dim).reshape(shape)


def moved_by_axis(parts, axes, sequence):
    inside = parts.shape[1:]
    result = parts.reshape(*(lax.axis_size(a) for a in axes), *inside)
    for k in sequence:
        result = lax.all_to_all(result, axes[k], k, k, tiled=True)
    return result.reshape(-1, *inside)


def core_and_chips(value, groups, sequence, split_dim, concat_dim):
    peers = lax.axis_size(groups[0]) * lax.axis_size(groups[1])
    parts = split_up(value, split_dim, peers)
    return joined_along(moved_by_axis(parts, groups, sequence), concat_dim)


def along_first(field):
    planes, xsize, ysize = field.shape
    blocks = np.kron(np.eye(xsize // GLL), np.array(deriv_table))
    table = jnp.asarray(blocks, jnp.float32)
    return jnp.einsum("ik,aky->aiy", table, field, precision=lax.Precision.HIGHEST)


def along_second(field):
    planes, xsize, ysize = field.shape
    width = min(ysize, 128)
    blocks = np.kron(np.eye(width // GLL), np.array(deriv_table).T)
    table = jnp.asarray(blocks, jnp.float32)
    shaped = field.reshape(planes, xsize, ysize // width, width)
    result = jnp.einsum("axek,ki->axei", shaped, table, precision=lax.Precision.HIGHEST)
    return result.reshape(planes, xsize, ysize)


def sum_rows(widened):
    xsize = widened.shape[1] - 2
    x_pos = jnp.arange(xsize, dtype=jnp.int32) % GLL
    first_row = (x_pos == 0)[:, None]
    last_row = (x_pos == GLL - 1)[:, None]
    return (
        widened[:, 1:-1]
        + jnp.where(first_row, widened[:, :-2], 0.0)
        + jnp.where(last_row, widened[:, 2:], 0.0)
    )


def sum_cols(widened):
    ysize = widened.shape[2] - 2
    y_pos = jnp.arange(ysize, dtype=jnp.int32) % GLL
    first_col = y_pos == 0
    last_col = y_pos == GLL - 1
    return (
        widened[:, :, 1:-1]
        + jnp.where(first_col, widened[:, :, :-2], 0.0)
        + jnp.where(last_col, widened[:, :, 2:], 0.0)
    )


def edge_average(moved, mass_map):
    weighted = jnp.concatenate([mass_map[None] * moved, mass_map[None]], axis=0)
    widened = with_halo(weighted, (("face", 1),), 1)
    partial_sum = sum_rows(widened)
    widened_cols = with_halo(partial_sum, ((BLK, 2),), 1)
    summed = sum_cols(widened_cols)
    return summed[:-1] / summed[-1:]


def lane_gather(rows, idx):
    hi = lax.shift_right_logical(idx, 7)
    lo = lax.bitwise_and(idx, 127)
    found = jnp.zeros(idx.shape, jnp.float32)
    for h, row in enumerate(rows):
        picked = jnp.take_along_axis(jnp.broadcast_to(row, idx.shape), lo, axis=1)
        found = jnp.where(hi == h, picked, found)
    return found


def gather_kernel(table_ref, idx_ref, out_ref):
    rows = [table_ref[h : h + 1, :] for h in range(table_ref.shape[0])]
    for i in range(idx_ref.shape[0] // 8):
        out_ref[8 * i : 8 * i + 8, :] = lane_gather(rows, idx_ref[8 * i : 8 * i + 8, :])


def gather_points(table, idx):
    return pl.pallas_call(
        gather_kernel, out_shape=jax.ShapeDtypeStruct(idx.shape, jnp.float32), name="gather_points"
    )(table, idx)


def lateral_kernel(ext_ref, near_ref, coef_ref, out_ref):
    planes, width = ext_ref.shape
    groups = planes // 8

    def block(j, carry):
        here = pl.ds(pl.multiple_of(j * 128, 128), 128)
        own = [ext_ref[8 * g : 8 * g + 8, here] for g in range(groups)]
        lateral = [jnp.zeros((8, 128), jnp.float32) for g in range(groups)]
        for e in range(near_ref.shape[0]):
            idx = jnp.broadcast_to(near_ref[e : e + 1, here], (8, 128))
            coef = jnp.broadcast_to(coef_ref[e : e + 1, here], (8, 128))
            hi = lax.shift_right_logical(idx, 7)
            lo = lax.bitwise_and(idx, 127)
            found = [jnp.zeros((8, 128), jnp.float32) for g in range(groups)]
            for h in range(width // 128):
                mine = hi == h
                for g in range(groups):
                    tile = ext_ref[8 * g : 8 * g + 8, 128 * h : 128 * h + 128]
                    found[g] = jnp.where(mine, jnp.take_along_axis(tile, lo, axis=1), found[g])
            for g in range(groups):
                lateral[g] = lateral[g] + coef * (found[g] - own[g])
        for g in range(groups):
            out_ref[8 * g : 8 * g + 8, here] = lateral[g]
        return carry

    lax.fori_loop(0, out_ref.shape[1] // 128, block, 0)


def scatter_kernel(idx_ref, *refs):
    value_refs, out_ref = refs[:-1], refs[-1]
    rows = out_ref.shape[1]
    lane_iota = lax.broadcasted_iota(jnp.int32, (128, 128), 0)
    row_iota = lax.broadcasted_iota(jnp.int32, (rows, 128), 0)

    def slots(r, total):
        idx = idx_ref[pl.ds(r, 1), :]
        lo = jnp.broadcast_to(lax.bitwise_and(idx, 127), (128, 128))
        hot = jnp.where(lane_iota == lo, 1.0, 0.0).astype(jnp.bfloat16)
        mine = jnp.broadcast_to(lax.shift_right_logical(idx, 7), (rows, 128)) == row_iota
        parts = []
        for ref in value_refs:
            rest = jnp.where(mine, jnp.broadcast_to(ref[pl.ds(r, 1), :], (rows, 128)), 0.0)
            for _ in range(3):
                part = rest.astype(jnp.bfloat16)
                parts.append(part)
                rest = rest - part.astype(jnp.float32)
        left = jnp.concatenate(parts, axis=0)
        return total + lax.dot_general(
            left, hot, (((1,), (1,)), ((), ())), preferred_element_type=jnp.float32
        )

    count = len(value_refs)
    total = lax.fori_loop(
        0, idx_ref.shape[0], slots, jnp.zeros((3 * count * rows, 128), jnp.float32)
    )
    for q in range(count):
        first = 3 * q * rows
        out_ref[q] = (
            total[first : first + rows]
            + total[first + rows : first + 2 * rows]
            + total[first + 2 * rows : first + 3 * rows]
        )


def scatter_points(idx, values, rows):
    return pl.pallas_call(
        scatter_kernel,
        out_shape=jax.ShapeDtypeStruct((len(values), rows, 128), jnp.float32),
        name="scatter_points",
    )(idx, *values)


def body(
    air_state,
    air_wind,
    jacobian,
    land_area,
    xgrid_rows,
    tracers,
    edge_coef,
    neighbours,
    vert_rate,
    ocean_area,
    send_list,
    xgrid_cols,
    xgrid_weights,
):
    field_count, levels, x_points, y_points = air_state.shape
    planes = field_count * levels
    cell_count = tracers.shape[2]
    send_ids = send_list[0]
    rim_width = send_ids.shape[0] // 2
    outgoing = tracers[:, :, send_ids]
    received = with_halo(outgoing, ((BLK, 2),), rim_width)
    extended = jnp.concatenate(
        [tracers, received[:, :, :rim_width], received[:, :, 3 * rim_width :]], axis=2
    )
    lateral = pl.pallas_call(
        lateral_kernel,
        out_shape=jax.ShapeDtypeStruct((tracers.shape[0] * tracers.shape[1], cell_count), jnp.float32),
        name="lateral",
    )(extended.reshape(-1, extended.shape[2]), neighbours, edge_coef).reshape(tracers.shape)
    upper_level = jnp.concatenate([tracers[:, :1], tracers[:, :-1]], axis=1)
    lower_level = jnp.concatenate([tracers[:, 1:], tracers[:, -1:]], axis=1)
    vertical = vert_rate * (upper_level - tracers + (lower_level - tracers))
    ocean_partial = tracers + lateral + vertical
    cell_ids = xgrid_cols[0]
    weights = xgrid_weights[0]
    surface_at = gather_points(tracers[0, 0].reshape(-1, 128), cell_ids)
    payload = jnp.stack([weights * surface_at, weights])
    arrived = core_and_chips(payload, (("blk_0", "blk_1"), "blk_2"), (0, 1), 1, 1)
    sums = scatter_points(xgrid_rows[0], (arrived[0], arrived[1]), x_points)
    heat_map = sums[0].reshape(x_points, y_points)
    frac_map = sums[1].reshape(x_points, y_points)
    t_surf = (heat_map + land_area * air_state[0, 0]) / (frac_map + land_area)
    x_pos = jnp.arange(x_points, dtype=jnp.int32) % GLL
    y_pos = jnp.arange(y_points, dtype=jnp.int32) % GLL
    x_weight = jnp.where((x_pos == 0) | (x_pos == GLL - 1), 1.0 / 6.0, 5.0 / 6.0).astype(
        jnp.float32
    )
    y_weight = jnp.where((y_pos == 0) | (y_pos == GLL - 1), 1.0 / 6.0, 5.0 / 6.0).astype(
        jnp.float32
    )
    mass_map = x_weight[:, None] * y_weight[None, :] * jacobian
    fields = air_state
    for substep in range(SUBSTEPS):
        flat_fields = fields.reshape(planes, x_points, y_points)
        slope_first = along_first(flat_fields).reshape(field_count, levels, x_points, y_points)
        slope_second = along_second(flat_fields).reshape(field_count, levels, x_points, y_points)
        tendency = -(air_wind[0] * slope_first + air_wind[1] * slope_second)
        moved = fields + time_step * tendency
        moved = moved.at[0, 0].add(relax_rate * (t_surf - fields[0, 0]))
        fields = edge_average(moved.reshape(planes, x_points, y_points), mass_map).reshape(
            field_count, levels, x_points, y_points
        )
    sea_flux = fields[0, 0] - t_surf
    flux_slots = gather_points(sea_flux, xgrid_rows[0])
    incoming = core_and_chips(flux_slots, (("blk_0", "blk_1"), "blk_2"), (1, 0), 0, 0)
    inflow = scatter_points(cell_ids, (weights * incoming,), cell_count // 128).reshape(-1)
    ocean_final = ocean_partial.at[0, 0].add(flux_gain * inflow / ocean_area)
    return (fields, ocean_final)


def solution(mesh):
    finer = Mesh(
        mesh.devices.reshape(mesh.shape["face"], 8, 4, 2), ("face", "blk_0", "blk_1", "blk_2")
    )
    in_specs = (
        P(None, None, "face", BLK),
        P(None, None, "face", BLK),
        P("face", BLK),
        P("face", BLK),
        P(FACE_BLK, None, None),
        P(None, None, FACE_BLK),
        P(None, FACE_BLK),
        P(None, FACE_BLK),
        P(FACE_BLK),
        P(FACE_BLK),
        P(FACE_BLK, None),
        P(FACE_BLK, None, None),
        P(FACE_BLK, None, None),
    )
    out_specs = (P(None, None, "face", BLK), P(None, None, FACE_BLK))
    return jax.shard_map(body, mesh=finer, in_specs=in_specs, out_specs=out_specs, check_vma=False)
```

```python
import jax
import jax.numpy as jnp
from jax import lax
from jax.experimental import pallas as pl
from jax.experimental.pallas import tpu as pltpu
from jax.sharding import PartitionSpec as P

GLL = 4
DERIV = (
    (-3.0, 4.045084971874737, -1.545084971874737, 0.5),
    (-0.8090169943749475, 0.0, 1.118033988749895, -0.30901699437494745),
    (0.30901699437494745, -1.118033988749895, 0.0, 0.8090169943749475),
    (-0.5, 1.545084971874737, -4.045084971874737, 3.0),
)
TIME_STEP = 0.05
RELAX = 0.3
FLUX_GAIN = 0.2
DIRECTIONS = ((-1, 0), (1, 0), (0, -1), (0, 1), (-1, -1), (-1, 1), (1, -1), (1, 1))
REVERSE = (1, 0, 3, 2, 7, 6, 5, 4)
MARGIN_ROWS = {-1: (0, 8), 1: (8, 16), 0: (0, 16)}
MESH = pl.DeviceIdType.MESH
F32 = jnp.float32
BF16 = jnp.bfloat16
TILE = (8, 128)


def lane_gather(rows, hi, lo):
    found = jnp.zeros(TILE, F32)
    for h, row in enumerate(rows):
        found = jnp.where(hi == h, jnp.take_along_axis(row, lo, axis=1), found)
    return found


def tap_table(position, shift):
    table = jnp.zeros(TILE, F32)
    for i in range(GLL):
        if 0 <= i + shift < GLL:
            table = jnp.where(position == i, F32(DERIV[i][i + shift]), table)
    return table


def build_hot(idx_ref, hot_ref):
    rows = lax.broadcasted_iota(jnp.int32, (128, 128), 0)

    def step(r8, carry):
        base = pl.multiple_of(r8 * 8, 8)
        for i in range(8):
            lo = lax.bitwise_and(idx_ref[pl.ds(base + i, 1), :], 127)
            hot = jnp.where(rows == jnp.broadcast_to(lo, (128, 128)), 1.0, 0.0).astype(BF16)
            hot_ref[:, pl.ds(pl.multiple_of((base + i) * 128, 128), 128)] = hot
        return carry

    lax.fori_loop(0, idx_ref.shape[0] // 8, step, 0)


def build_left(idx_ref, values_at, left_ref):
    rows = lax.broadcasted_iota(jnp.int32, (16, 128), 0)

    def step(r8, carry):
        base = pl.multiple_of(r8 * 8, 8)
        hi = lax.shift_right_logical(idx_ref[pl.ds(base, 8), :], 7)
        parts = []
        for rest in values_at(base):
            for _ in range(3):
                part = rest.astype(BF16).astype(F32)
                parts.append(part)
                rest = rest - part
        for i in range(8):
            mine = jnp.broadcast_to(hi[i : i + 1], (16, 128)) == rows
            left = [
                jnp.where(mine, jnp.broadcast_to(p[i : i + 1], (16, 128)), 0.0).astype(BF16)
                for p in parts
            ]
            left_ref[0 : 16 * len(parts), pl.ds(pl.multiple_of((base + i) * 128, 128), 128)] = (
                jnp.concatenate(left, axis=0)
            )
        return carry

    lax.fori_loop(0, idx_ref.shape[0] // 8, step, 0)


def scatter_sums(left_ref, hot_ref, count):
    total = lax.dot_general(
        left_ref[0 : 48 * count, :],
        hot_ref[...],
        (((1,), (1,)), ((), ())),
        preferred_element_type=F32,
    )
    return [
        total[48 * q : 48 * q + 16] + total[48 * q + 16 : 48 * q + 32] + total[48 * q + 32 : 48 * q + 48]
        for q in range(count)
    ]


def interval_kernel(
    n_face,
    n_blk,
    air_ref,
    wind_ref,
    jac_ref,
    land_ref,
    rows_ref,
    tracer_ref,
    coef_ref,
    near_ref,
    vert_ref,
    area_ref,
    send_ref,
    cols_ref,
    weight_ref,
    air_out,
    ocean_out,
    heat_pay,
    heat_in,
    flux_pay,
    flux_in,
    rim_pay,
    rim_in,
    margin_pay,
    margin_in,
    surf_pay,
    surf_in,
    weighted_1,
    weighted_2,
    row_sum,
    column_pay_1,
    column_in_1,
    column_pay_2,
    column_in_2,
    field_1,
    mass_ref,
    inverse_ref,
    hot_rows,
    hot_cols,
    left_ref,
    base_ref,
    wide_ref,
    all_send,
    all_recv,
    near_send,
    near_recv,
):
    face, blk = lax.axis_index("face"), lax.axis_index("blk")

    def step_to(d):
        df, db = DIRECTIONS[d]
        return (lax.rem(face + df + n_face, n_face), lax.rem(blk + db + n_blk, n_blk))

    barrier = pltpu.get_barrier_semaphore()

    def greet(k, carry):
        peer = lax.rem(blk + k, n_blk)
        pl.semaphore_signal(barrier, inc=1, device_id=(face, peer), device_id_type=MESH)
        return carry

    lax.fori_loop(1, n_blk, greet, 0)
    for d in (0, 1, 4, 5, 6, 7):
        pl.semaphore_signal(barrier, inc=1, device_id=step_to(d), device_id_type=MESH)

    sub = lax.broadcasted_iota(jnp.int32, TILE, 0)
    lane = lax.broadcasted_iota(jnp.int32, TILE, 1)
    x_pos, y_pos = lax.bitwise_and(sub, 3), lax.bitwise_and(lane, 3)
    first_x, last_x = x_pos == 0, x_pos == 3
    first_y, last_y = y_pos == 0, y_pos == 3
    sixth, five_sixths = F32(1.0 / 6.0), F32(5.0 / 6.0)
    gll_weight = jnp.where(first_x | last_x, sixth, five_sixths) * jnp.where(
        first_y | last_y, sixth, five_sixths
    )
    shifts = (-3, -2, -1, 1, 2, 3)

    surface = [
        jnp.broadcast_to(tracer_ref[0:1, 128 * h : 128 * h + 128], TILE) for h in range(16)
    ]
    for i in range(n_blk // 8):
        idx = cols_ref[8 * i : 8 * i + 8, :]
        weight = weight_ref[8 * i : 8 * i + 8, :]
        at = lane_gather(surface, lax.shift_right_logical(idx, 7), lax.bitwise_and(idx, 127))
        heat_pay[8 * i : 8 * i + 8, 0, :] = weight * at
        heat_pay[8 * i : 8 * i + 8, 1, :] = weight

    for side in range(2):
        idx = jnp.broadcast_to(send_ref[side : side + 1, :], TILE)
        hi, lo = lax.shift_right_logical(idx, 7), lax.bitwise_and(idx, 127)
        for g in range(4):
            tiles = [tracer_ref[8 * g : 8 * g + 8, 128 * h : 128 * h + 128] for h in range(16)]
            rim_pay[side, 8 * g : 8 * g + 8, :] = lane_gather(tiles, hi, lo)

    margin_pay[0] = air_ref[0:16, :]
    margin_pay[1] = wind_ref[0:16, :]
    margin_pay[2] = wind_ref[256:272, :]
    margin_pay[3] = jac_ref[...]
    for half in range(2):
        mass_ref[8 * half : 8 * half + 8, :] = gll_weight * jac_ref[8 * half : 8 * half + 8, :]

    taps_y = [(s, tap_table(y_pos, s)) for s in shifts]
    centre_y = tap_table(y_pos, 0)

    def slope_y(v):
        total = centre_y * v
        for s, tap in taps_y:
            total = total + tap * pltpu.roll(v, (-s) % 128, 1)
        return total

    def advance(field_at, target):
        def group(g, carry):
            half = lax.rem(g, 2) * 128
            planes = pl.ds(pl.multiple_of(g * 8, 8), 8)
            for e in range(4):
                fields = [field_at(g, 4 * e + k) for k in range(4)]
                for i in range(4):
                    x = 4 * e + i
                    slope_x = None
                    for k in range(4):
                        if DERIV[i][k]:
                            term = F32(DERIV[i][k]) * fields[k]
                            slope_x = term if slope_x is None else slope_x + term
                    wind_x = wind_ref[pl.ds(half + x, 8, stride=16), :]
                    wind_y = wind_ref[pl.ds(half + 256 + x, 8, stride=16), :]
                    tendency = wind_x * slope_x + wind_y * slope_y(fields[i])
                    moved = fields[i] - F32(TIME_STEP) * tendency
                    mass = jnp.broadcast_to(mass_ref[x : x + 1, :], TILE)
                    target[x + 1, planes, :] = mass * moved
            return carry

        lax.fori_loop(0, 6, group, 0)

    advance(lambda g, x: air_ref[pl.ds(g * 128 + x, 8, stride=16), :], weighted_1)
    build_hot(rows_ref, hot_rows)

    pl.semaphore_wait(barrier, n_blk - 1 + 6)

    def exchange(pay, inbox, slot):
        def send(k, carry):
            peer = lax.rem(blk + k, n_blk)
            pltpu.make_async_remote_copy(
                src_ref=pay.at[peer],
                dst_ref=inbox.at[blk],
                send_sem=all_send.at[slot],
                recv_sem=all_recv.at[slot],
                device_id=(face, peer),
                device_id_type=MESH,
            ).start()
            return carry

        lax.fori_loop(1, n_blk, send, 0)

    def await_all(ref, sem):
        rest = ref.at[pl.ds(0, n_blk - 1)]
        pltpu.make_async_copy(rest, rest, sem).wait()

    started = []

    def send_near(src, dst, d, slot):
        copy = pltpu.make_async_remote_copy(
            src_ref=src,
            dst_ref=dst,
            send_sem=near_send.at[slot],
            recv_sem=near_recv.at[slot],
            device_id=step_to(d),
            device_id_type=MESH,
        )
        copy.start()
        started.append(copy)
        return copy

    exchange(heat_pay, heat_in, 0)
    margin_copies, surf_copies = [], []
    for d in range(8):
        low, high = MARGIN_ROWS[DIRECTIONS[d][0]]
        margin_copies.append(
            send_near(
                margin_pay.at[:, low:high, :],
                margin_in.at[REVERSE[d], :, 0 : high - low, :],
                d,
                d,
            )
        )
    row_copies = [
        send_near(weighted_1.at[1], weighted_1.at[17], 0, 16),
        send_near(weighted_1.at[16], weighted_1.at[0], 1, 17),
    ]
    rim_copies = [
        send_near(rim_pay.at[0], rim_in.at[1], 2, 24),
        send_near(rim_pay.at[1], rim_in.at[0], 3, 25),
    ]
    heat_in[blk] = heat_pay[blk]

    def ocean(first, last):
        def block(j, carry):
            here = pl.ds(pl.multiple_of(j * 128, 128), 128)
            own = [tracer_ref[8 * g : 8 * g + 8, here] for g in range(4)]
            lateral = [jnp.zeros(TILE, F32) for g in range(4)]
            for e in range(6):
                idx = jnp.broadcast_to(near_ref[e : e + 1, here], TILE)
                coef = jnp.broadcast_to(coef_ref[e : e + 1, here], TILE)
                hi, lo = lax.shift_right_logical(idx, 7), lax.bitwise_and(idx, 127)
                found = [jnp.zeros(TILE, F32) for g in range(4)]
                for h in range(18):
                    mine = hi == h
                    for g in range(4):
                        if h < 16:
                            tile = tracer_ref[8 * g : 8 * g + 8, 128 * h : 128 * h + 128]
                        else:
                            tile = rim_in[h - 16, 8 * g : 8 * g + 8, :]
                        found[g] = jnp.where(mine, jnp.take_along_axis(tile, lo, axis=1), found[g])
                for g in range(4):
                    lateral[g] = lateral[g] + coef * (found[g] - own[g])
            rate = jnp.broadcast_to(vert_ref[pl.ds(j, 1), :], TILE)
            for t in range(2):
                top, low = own[2 * t], own[2 * t + 1]
                down = [pltpu.roll(v, 1, 0) for v in (top, low)]
                up = [pltpu.roll(v, 7, 0) for v in (top, low)]
                above = [jnp.where(sub == 0, top, down[0]), jnp.where(sub == 0, down[0], down[1])]
                below = [jnp.where(sub == 7, up[1], up[0]), jnp.where(sub == 7, low, up[1])]
                for i, v in enumerate((top, low)):
                    g = 2 * t + i
                    vertical = rate * ((above[i] - v) + (below[i] - v))
                    ocean_out[8 * g : 8 * g + 8, here] = v + lateral[g] + vertical
            return carry

        lax.fori_loop(first, last, block, 0)

    def sum_rows(weighted, column_pay):
        def group(g, carry):
            planes = pl.ds(pl.multiple_of(g * 8, 8), 8)
            packed = [jnp.zeros(TILE, F32), jnp.zeros(TILE, F32)]
            for x in range(16):
                total = weighted[x + 1, planes, :]
                if x % 4 == 0:
                    total = total + weighted[x, planes, :]
                if x % 4 == 3:
                    total = total + weighted[x + 2, planes, :]
                row_sum[x, planes, :] = total
                packed[0] = jnp.where(lane == x, pltpu.roll(total, x, 1), packed[0])
                packed[1] = jnp.where(lane == x, pltpu.roll(total, x + 1, 1), packed[1])
            for side in range(2):
                column_pay[side, planes, :] = packed[side]
            return carry

        lax.fori_loop(0, 6, group, 0)

    def sum_columns(column_in, store):
        def group(g, carry):
            planes = pl.ds(pl.multiple_of(g * 8, 8), 8)
            left, right = column_in[0, planes, :], column_in[1, planes, :]
            for x in range(16):
                v = row_sum[x, planes, :]
                before = jnp.where(
                    lane == 0, pltpu.roll(left, (128 - x) % 128, 1), pltpu.roll(v, 1, 1)
                )
                after = jnp.where(
                    lane == 127, pltpu.roll(right, 127 - x, 1), pltpu.roll(v, 127, 1)
                )
                total = v + jnp.where(first_y, before, 0.0) + jnp.where(last_y, after, 0.0)
                store(g, x, total * jnp.broadcast_to(inverse_ref[x : x + 1, :], TILE))
            return carry

        lax.fori_loop(0, 6, group, 0)

    for copy in row_copies:
        copy.wait_recv()
    sum_rows(weighted_1, column_pay_1)
    column_copies = [
        send_near(column_pay_1.at[0], column_in_1.at[1], 2, 18),
        send_near(column_pay_1.at[1], column_in_1.at[0], 3, 19),
    ]

    for copy in margin_copies:
        copy.wait_recv()

    def widen(own, inbox):
        centre = [own[0:8], own[8:16], inbox(1)[0:8], inbox(0)[0:8]]
        right = [inbox(3)[0:8], inbox(3)[8:16], inbox(7)[0:8], inbox(5)[0:8]]
        left = [inbox(2)[0:8], inbox(2)[8:16], inbox(6)[0:8], inbox(4)[0:8]]
        return centre + [jnp.where(lane < 64, r, l) for r, l in zip(right, left)]

    def copy_sum(tiles):
        summed = []
        for side in range(2):
            part = tiles[4 * side : 4 * side + 4]
            prev = [pltpu.roll(v, 1, 0) for v in part]
            succ = [pltpu.roll(v, 7, 0) for v in part]
            for i in range(4):
                before = jnp.where(sub == 0, prev[i - 1], prev[i])
                after = jnp.where(sub == 7, succ[(i + 1) % 4], succ[i])
                summed.append(
                    part[i] + jnp.where(first_x, before, 0.0) + jnp.where(last_x, after, 0.0)
                )
        prev = [pltpu.roll(v, 1, 1) for v in summed]
        succ = [pltpu.roll(v, 127, 1) for v in summed]
        result = []
        for i in range(8):
            other = (i + 4) % 8
            before = jnp.where(lane == 0, prev[other], prev[i])
            after = jnp.where(lane == 127, succ[other], succ[i])
            result.append(
                summed[i] + jnp.where(first_y, before, 0.0) + jnp.where(last_y, after, 0.0)
            )
        return result

    taps_x = [(s, tap_table(x_pos, s)) for s in shifts]
    centre_x = tap_table(x_pos, 0)

    def without_surface(v, wind_x, wind_y):
        slope_x = centre_x * v
        for s, tap in taps_x:
            slope_x = slope_x + tap * pltpu.roll(v, (-s) % 8, 0)
        return v - F32(TIME_STEP) * (wind_x * slope_x + wind_y * slope_y(v)) - F32(RELAX) * v

    wide = [
        widen(margin_pay[q], lambda d, q=q: margin_in[d, q]) for q in range(4)
    ]
    wide_mass = [gll_weight * v for v in wide[3]]
    wide_inverse = [1.0 / v for v in copy_sum(wide_mass)]
    for i in range(8):
        base_ref[i] = without_surface(wide[0][i], wide[1][i], wide[2][i])
        wide_ref[0, i] = wide[1][i]
        wide_ref[1, i] = wide[2][i]
        wide_ref[2, i] = wide_mass[i]
        wide_ref[3, i] = wide_inverse[i]
    for half in range(2):
        inverse_ref[8 * half : 8 * half + 8, :] = wide_inverse[half]

    for copy in column_copies:
        copy.wait_recv()

    def keep(g, x, v):
        field_1[x, pl.ds(pl.multiple_of(g * 8, 8), 8), :] = v

    sum_columns(column_in_1, keep)
    advance(lambda g, x: field_1[x, pl.ds(pl.multiple_of(g * 8, 8), 8), :], weighted_2)
    row_copies = [
        send_near(weighted_2.at[1], weighted_2.at[17], 0, 20),
        send_near(weighted_2.at[16], weighted_2.at[0], 1, 21),
    ]

    await_all(heat_in, all_recv.at[0])
    build_left(
        rows_ref,
        lambda base: (heat_in[pl.ds(base, 8), 0, :], heat_in[pl.ds(base, 8), 1, :]),
        left_ref,
    )
    heat, frac = scatter_sums(left_ref, hot_rows, 2)
    surf_pay[...] = (heat + land_ref[...] * air_ref[0:16, :]) / (frac + land_ref[...])
    for d in range(8):
        low, high = MARGIN_ROWS[DIRECTIONS[d][0]]
        surf_copies.append(
            send_near(
                surf_pay.at[low:high, :],
                surf_in.at[REVERSE[d], 0 : high - low, :],
                d,
                8 + d,
            )
        )

    for copy in row_copies:
        copy.wait_recv()
    sum_rows(weighted_2, column_pay_2)
    column_copies = [
        send_near(column_pay_2.at[0], column_in_2.at[1], 2, 22),
        send_near(column_pay_2.at[1], column_in_2.at[0], 3, 23),
    ]

    for copy in surf_copies:
        copy.wait_recv()
    surf = widen(surf_pay[...], lambda d: surf_in[d])
    moved = [
        wide_ref[2, i] * (base_ref[i] + F32(RELAX) * surf[i]) for i in range(8)
    ]
    field = [v * wide_ref[3, i] for i, v in enumerate(copy_sum(moved))]
    moved = [
        wide_ref[2, i]
        * (without_surface(field[i], wide_ref[0, i], wide_ref[1, i]) + F32(RELAX) * surf[i])
        for i in range(8)
    ]
    final = [v * wide_ref[3, i] for i, v in enumerate(copy_sum(moved)[0:2])]
    flux = [
        jnp.broadcast_to((final[h // 8] - surf[h // 8])[h % 8 : h % 8 + 1], TILE)
        for h in range(16)
    ]
    for i in range(n_blk // 8):
        idx = rows_ref[8 * i : 8 * i + 8, :]
        flux_pay[8 * i : 8 * i + 8, 0, :] = lane_gather(
            flux, lax.shift_right_logical(idx, 7), lax.bitwise_and(idx, 127)
        )
    exchange(flux_pay, flux_in, 1)
    flux_in[blk] = flux_pay[blk]

    for copy in column_copies:
        copy.wait_recv()

    def put_out(g, x, v):
        air_out[pl.ds(g * 128 + x, 8, stride=16), :] = v

    sum_columns(column_in_2, put_out)
    for half in range(2):
        air_out[8 * half : 8 * half + 8, :] = final[half]
    build_hot(cols_ref, hot_cols)
    for copy in rim_copies:
        copy.wait_recv()
    ocean(0, 16)

    await_all(flux_in, all_recv.at[1])
    build_left(
        cols_ref,
        lambda base: (weight_ref[pl.ds(base, 8), :] * flux_in[pl.ds(base, 8), 0, :],),
        left_ref,
    )
    (inflow,) = scatter_sums(left_ref, hot_cols, 1)
    gain = F32(FLUX_GAIN) * inflow / area_ref[...]
    for h in range(16):
        here = slice(128 * h, 128 * h + 128)
        ocean_out[0:1, here] = ocean_out[0:1, here] + gain[h : h + 1]

    for copy in started:
        copy.wait_send()
    await_all(heat_pay, all_send.at[0])
    await_all(flux_pay, all_send.at[1])


def solution(mesh):
    n_face, n_blk = mesh.shape["face"], mesh.shape["blk"]

    def body(
        air_state,
        air_wind,
        jacobian,
        land_area,
        xgrid_rows,
        tracers,
        edge_coef,
        neighbours,
        vert_rate,
        ocean_area,
        send_list,
        xgrid_cols,
        xgrid_weights,
    ):
        air_shape, ocean_shape = air_state.shape, tracers.shape
        vmem = pltpu.VMEM
        air, ocean = pl.pallas_call(
            lambda *refs: interval_kernel(n_face, n_blk, *refs),
            out_shape=(
                jax.ShapeDtypeStruct((768, 128), F32),
                jax.ShapeDtypeStruct((32, 2048), F32),
            ),
            in_specs=[pl.BlockSpec(memory_space=vmem)] * 13,
            out_specs=(pl.BlockSpec(memory_space=vmem),) * 2,
            scratch_shapes=[
                vmem((n_blk, 2, 128), F32),
                vmem((n_blk, 2, 128), F32),
                vmem((n_blk, 1, 128), F32),
                vmem((n_blk, 1, 128), F32),
                vmem((2, 32, 128), F32),
                vmem((2, 32, 128), F32),
                vmem((4, 16, 128), F32),
                vmem((8, 4, 16, 128), F32),
                vmem((16, 128), F32),
                vmem((8, 16, 128), F32),
                vmem((18, 48, 128), F32),
                vmem((18, 48, 128), F32),
                vmem((16, 48, 128), F32),
                vmem((2, 48, 128), F32),
                vmem((2, 48, 128), F32),
                vmem((2, 48, 128), F32),
                vmem((2, 48, 128), F32),
                vmem((16, 48, 128), F32),
                vmem((16, 128), F32),
                vmem((16, 128), F32),
                vmem((128, 128 * n_blk), BF16),
                vmem((128, 128 * n_blk), BF16),
                vmem((96, 128 * n_blk), BF16),
                vmem((8, 8, 128), F32),
                vmem((4, 8, 8, 128), F32),
                pltpu.SemaphoreType.DMA((2,)),
                pltpu.SemaphoreType.DMA((2,)),
                pltpu.SemaphoreType.DMA((26,)),
                pltpu.SemaphoreType.DMA((26,)),
            ],
            compiler_params=pltpu.CompilerParams(collective_id=0, has_side_effects=True),
            name="interval",
        )(
            air_state.reshape(768, 128),
            air_wind.reshape(512, 128),
            jacobian,
            land_area,
            xgrid_rows[0],
            tracers.reshape(32, 2048),
            edge_coef,
            neighbours,
            vert_rate.reshape(16, 128),
            ocean_area.reshape(16, 128),
            send_list.reshape(2, 128),
            xgrid_cols[0],
            xgrid_weights[0],
        )
        return air.reshape(air_shape), ocean.reshape(ocean_shape)

    both = ("face", "blk")
    in_specs = (
        P(None, None, "face", "blk"),
        P(None, None, "face", "blk"),
        P("face", "blk"),
        P("face", "blk"),
        P(both, None, None),
        P(None, None, both),
        P(None, both),
        P(None, both),
        P(both),
        P(both),
        P(both, None),
        P(both, None, None),
        P(both, None, None),
    )
    out_specs = (P(None, None, "face", "blk"), P(None, None, both))
    return jax.shard_map(body, mesh=mesh, in_specs=in_specs, out_specs=out_specs, check_vma=False)
```

```python
import jax
import jax.numpy as jnp
from jax import lax
from jax.experimental import pallas as pl
from jax.experimental.pallas import tpu as pltpu
from jax.sharding import PartitionSpec as P

GLL = 4
DERIV = (
    (-3.0, 4.045084971874737, -1.545084971874737, 0.5),
    (-0.8090169943749475, 0.0, 1.118033988749895, -0.30901699437494745),
    (0.30901699437494745, -1.118033988749895, 0.0, 0.8090169943749475),
    (-0.5, 1.545084971874737, -4.045084971874737, 3.0),
)
TIME_STEP = 0.05
RELAX = 0.3
FLUX_GAIN = 0.2
DIRECTIONS = ((-1, 0), (1, 0), (0, -1), (0, 1), (-1, -1), (-1, 1), (1, -1), (1, 1))
REVERSE = (1, 0, 3, 2, 7, 6, 5, 4)
MARGIN_ROWS = {-1: (0, 8), 1: (8, 16), 0: (0, 16)}
MESH = pl.DeviceIdType.MESH
F32 = jnp.float32
BF16 = jnp.bfloat16
TILE = (8, 128)


def lane_gather(rows, hi, lo):
    found = jnp.zeros(TILE, F32)
    for h, row in enumerate(rows):
        found = jnp.where(hi == h, jnp.take_along_axis(row, lo, axis=1), found)
    return found


def tap_table(position, shift):
    table = jnp.zeros(TILE, F32)
    for i in range(GLL):
        if 0 <= i + shift < GLL:
            table = jnp.where(position == i, F32(DERIV[i][i + shift]), table)
    return table


def build_hot(idx_ref, hot_ref):
    rows = lax.broadcasted_iota(jnp.int32, (128, 128), 0)

    def step(r8, carry):
        base = pl.multiple_of(r8 * 8, 8)
        for i in range(8):
            lo = lax.bitwise_and(idx_ref[pl.ds(base + i, 1), :], 127)
            hot = jnp.where(rows == jnp.broadcast_to(lo, (128, 128)), 1.0, 0.0).astype(BF16)
            hot_ref[:, pl.ds(pl.multiple_of((base + i) * 128, 128), 128)] = hot
        return carry

    lax.fori_loop(0, idx_ref.shape[0] // 8, step, 0)


def build_left(idx_ref, values_at, left_ref):
    rows = lax.broadcasted_iota(jnp.int32, (16, 128), 0)

    def step(r8, carry):
        base = pl.multiple_of(r8 * 8, 8)
        hi = lax.shift_right_logical(idx_ref[pl.ds(base, 8), :], 7)
        parts = []
        for rest in values_at(base):
            for _ in range(3):
                part = rest.astype(BF16).astype(F32)
                parts.append(part)
                rest = rest - part
        for i in range(8):
            mine = jnp.broadcast_to(hi[i : i + 1], (16, 128)) == rows
            left = [
                jnp.where(mine, jnp.broadcast_to(p[i : i + 1], (16, 128)), 0.0).astype(BF16)
                for p in parts
            ]
            left_ref[0 : 16 * len(parts), pl.ds(pl.multiple_of((base + i) * 128, 128), 128)] = (
                jnp.concatenate(left, axis=0)
            )
        return carry

    lax.fori_loop(0, idx_ref.shape[0] // 8, step, 0)


def scatter_sums(left_ref, hot_ref, count):
    total = lax.dot_general(
        left_ref[0 : 48 * count, :],
        hot_ref[...],
        (((1,), (1,)), ((), ())),
        preferred_element_type=F32,
    )
    return [
        total[48 * q : 48 * q + 16] + total[48 * q + 16 : 48 * q + 32] + total[48 * q + 32 : 48 * q + 48]
        for q in range(count)
    ]


def interval_kernel(
    n_face,
    n_blk,
    air_hbm,
    wind_hbm,
    jac_hbm,
    land_hbm,
    rows_hbm,
    tracer_hbm,
    coef_hbm,
    near_hbm,
    vert_hbm,
    area_hbm,
    send_hbm,
    cols_hbm,
    weight_hbm,
    air_out,
    ocean_out,
    air_ref,
    wind_ref,
    jac_ref,
    land_ref,
    rows_ref,
    tracer_ref,
    coef_ref,
    near_ref,
    vert_ref,
    area_ref,
    send_ref,
    cols_ref,
    weight_ref,
    load_sem,
    heat_pay,
    heat_in,
    flux_pay,
    flux_in,
    rim_pay,
    rim_in,
    margin_pay,
    margin_in,
    surf_pay,
    surf_in,
    weighted_1,
    weighted_2,
    row_sum,
    column_pay_1,
    column_in_1,
    column_pay_2,
    column_in_2,
    field_1,
    mass_ref,
    inverse_ref,
    hot_rows,
    hot_cols,
    left_ref,
    base_ref,
    wide_ref,
    all_send,
    all_recv,
    near_send,
    near_recv,
):
    face, blk = lax.axis_index("face"), lax.axis_index("blk")

    def step_to(d):
        df, db = DIRECTIONS[d]
        return (lax.rem(face + df + n_face, n_face), lax.rem(blk + db + n_blk, n_blk))

    names = (
        *("cols", "weight", "tracer", "send", "air", "wind", "jac"),
        *("rows", "land", "coef", "near", "vert", "area"),
    )
    pairs = {
        "air": (air_hbm, air_ref),
        "wind": (wind_hbm, wind_ref),
        "jac": (jac_hbm, jac_ref),
        "land": (land_hbm, land_ref),
        "rows": (rows_hbm, rows_ref),
        "tracer": (tracer_hbm, tracer_ref),
        "coef": (coef_hbm, coef_ref),
        "near": (near_hbm, near_ref),
        "vert": (vert_hbm, vert_ref),
        "area": (area_hbm, area_ref),
        "send": (send_hbm, send_ref),
        "cols": (cols_hbm, cols_ref),
        "weight": (weight_hbm, weight_ref),
    }
    loads = {
        name: pltpu.make_async_copy(*pairs[name], load_sem.at[i]) for i, name in enumerate(names)
    }
    for name in names:
        loads[name].start()

    def loaded(*wanted):
        for name in wanted:
            loads[name].wait()

    def every_peer(act):
        half = n_blk // 2
        act(lax.rem(blk + half, n_blk))

        def both(k, carry):
            act(lax.rem(blk + half + k, n_blk))
            act(lax.rem(blk + half - k, n_blk))
            return carry

        lax.fori_loop(1, half, both, 0)

    barrier = pltpu.get_barrier_semaphore()
    for d in (4, 5, 6, 7, 0, 1):
        pl.semaphore_signal(barrier, inc=1, device_id=step_to(d), device_id_type=MESH)
    every_peer(
        lambda peer: pl.semaphore_signal(
            barrier, inc=1, device_id=(face, peer), device_id_type=MESH
        )
    )

    sub = lax.broadcasted_iota(jnp.int32, TILE, 0)
    lane = lax.broadcasted_iota(jnp.int32, TILE, 1)
    x_pos, y_pos = lax.bitwise_and(sub, 3), lax.bitwise_and(lane, 3)
    first_x, last_x = x_pos == 0, x_pos == 3
    first_y, last_y = y_pos == 0, y_pos == 3
    sixth, five_sixths = F32(1.0 / 6.0), F32(5.0 / 6.0)
    gll_weight = jnp.where(first_x | last_x, sixth, five_sixths) * jnp.where(
        first_y | last_y, sixth, five_sixths
    )
    shifts = (-3, -2, -1, 1, 2, 3)

    loaded("cols", "weight", "tracer")
    surface = [
        jnp.broadcast_to(tracer_ref[0:1, 128 * h : 128 * h + 128], TILE) for h in range(16)
    ]
    for i in range(n_blk // 8):
        idx = cols_ref[8 * i : 8 * i + 8, :]
        weight = weight_ref[8 * i : 8 * i + 8, :]
        at = lane_gather(surface, lax.shift_right_logical(idx, 7), lax.bitwise_and(idx, 127))
        heat_pay[8 * i : 8 * i + 8, 0, :] = weight * at
        heat_pay[8 * i : 8 * i + 8, 1, :] = weight

    pl.semaphore_wait(barrier, n_blk - 1 + 6)

    def exchange(pay, inbox, slot):
        every_peer(
            lambda peer: pltpu.make_async_remote_copy(
                src_ref=pay.at[peer],
                dst_ref=inbox.at[blk],
                send_sem=all_send.at[slot],
                recv_sem=all_recv.at[slot],
                device_id=(face, peer),
                device_id_type=MESH,
            ).start()
        )

    def await_all(ref, sem):
        rest = ref.at[pl.ds(0, n_blk - 1)]
        pltpu.make_async_copy(rest, rest, sem).wait()

    started = []

    def send_near(src, dst, d, slot):
        copy = pltpu.make_async_remote_copy(
            src_ref=src,
            dst_ref=dst,
            send_sem=near_send.at[slot],
            recv_sem=near_recv.at[slot],
            device_id=step_to(d),
            device_id_type=MESH,
        )
        copy.start()
        started.append(copy)
        return copy

    exchange(heat_pay, heat_in, 0)
    heat_in[blk] = heat_pay[blk]

    loaded("air", "wind", "jac")
    margin_pay[0] = air_ref[0:16, :]
    margin_pay[1] = wind_ref[0:16, :]
    margin_pay[2] = wind_ref[256:272, :]
    margin_pay[3] = jac_ref[...]
    for half in range(2):
        mass_ref[8 * half : 8 * half + 8, :] = gll_weight * jac_ref[8 * half : 8 * half + 8, :]

    margin_copies, surf_copies = [], []
    for d in range(8):
        low, high = MARGIN_ROWS[DIRECTIONS[d][0]]
        margin_copies.append(
            send_near(
                margin_pay.at[:, low:high, :],
                margin_in.at[REVERSE[d], :, 0 : high - low, :],
                d,
                d,
            )
        )

    loaded("send")
    for side in range(2):
        idx = jnp.broadcast_to(send_ref[side : side + 1, :], TILE)
        hi, lo = lax.shift_right_logical(idx, 7), lax.bitwise_and(idx, 127)
        for g in range(4):
            tiles = [tracer_ref[8 * g : 8 * g + 8, 128 * h : 128 * h + 128] for h in range(16)]
            rim_pay[side, 8 * g : 8 * g + 8, :] = lane_gather(tiles, hi, lo)

    rim_copies = [
        send_near(rim_pay.at[0], rim_in.at[1], 2, 24),
        send_near(rim_pay.at[1], rim_in.at[0], 3, 25),
    ]

    taps_y = [(s, tap_table(y_pos, s)) for s in shifts]
    centre_y = tap_table(y_pos, 0)

    def slope_y(v):
        total = centre_y * v
        for s, tap in taps_y:
            total = total + tap * pltpu.roll(v, (-s) % 128, 1)
        return total

    def advance(field_at, target):
        def group(g, carry):
            half = lax.rem(g, 2) * 128
            planes = pl.ds(pl.multiple_of(g * 8, 8), 8)
            for e in range(4):
                fields = [field_at(g, 4 * e + k) for k in range(4)]
                for i in range(4):
                    x = 4 * e + i
                    slope_x = None
                    for k in range(4):
                        if DERIV[i][k]:
                            term = F32(DERIV[i][k]) * fields[k]
                            slope_x = term if slope_x is None else slope_x + term
                    wind_x = wind_ref[pl.ds(half + x, 8, stride=16), :]
                    wind_y = wind_ref[pl.ds(half + 256 + x, 8, stride=16), :]
                    tendency = wind_x * slope_x + wind_y * slope_y(fields[i])
                    moved = fields[i] - F32(TIME_STEP) * tendency
                    mass = jnp.broadcast_to(mass_ref[x : x + 1, :], TILE)
                    target[x + 1, planes, :] = mass * moved
            return carry

        lax.fori_loop(0, 6, group, 0)

    advance(lambda g, x: air_ref[pl.ds(g * 128 + x, 8, stride=16), :], weighted_1)
    row_copies = [
        send_near(weighted_1.at[1], weighted_1.at[17], 0, 16),
        send_near(weighted_1.at[16], weighted_1.at[0], 1, 17),
    ]
    loaded("rows", "land", "coef", "near", "vert", "area")
    build_hot(rows_ref, hot_rows)

    def ocean(first, last):
        def block(j, carry):
            here = pl.ds(pl.multiple_of(j * 128, 128), 128)
            own = [tracer_ref[8 * g : 8 * g + 8, here] for g in range(4)]
            lateral = [jnp.zeros(TILE, F32) for g in range(4)]
            for e in range(6):
                idx = jnp.broadcast_to(near_ref[e : e + 1, here], TILE)
                coef = jnp.broadcast_to(coef_ref[e : e + 1, here], TILE)
                hi, lo = lax.shift_right_logical(idx, 7), lax.bitwise_and(idx, 127)
                found = [jnp.zeros(TILE, F32) for g in range(4)]
                for h in range(18):
                    mine = hi == h
                    for g in range(4):
                        if h < 16:
                            tile = tracer_ref[8 * g : 8 * g + 8, 128 * h : 128 * h + 128]
                        else:
                            tile = rim_in[h - 16, 8 * g : 8 * g + 8, :]
                        found[g] = jnp.where(mine, jnp.take_along_axis(tile, lo, axis=1), found[g])
                for g in range(4):
                    lateral[g] = lateral[g] + coef * (found[g] - own[g])
            rate = jnp.broadcast_to(vert_ref[pl.ds(j, 1), :], TILE)
            for t in range(2):
                top, low = own[2 * t], own[2 * t + 1]
                down = [pltpu.roll(v, 1, 0) for v in (top, low)]
                up = [pltpu.roll(v, 7, 0) for v in (top, low)]
                above = [jnp.where(sub == 0, top, down[0]), jnp.where(sub == 0, down[0], down[1])]
                below = [jnp.where(sub == 7, up[1], up[0]), jnp.where(sub == 7, low, up[1])]
                for i, v in enumerate((top, low)):
                    g = 2 * t + i
                    vertical = rate * ((above[i] - v) + (below[i] - v))
                    ocean_out[8 * g : 8 * g + 8, here] = v + lateral[g] + vertical
            return carry

        lax.fori_loop(first, last, block, 0)

    def sum_rows(weighted, column_pay):
        def group(g, carry):
            planes = pl.ds(pl.multiple_of(g * 8, 8), 8)
            packed = [jnp.zeros(TILE, F32), jnp.zeros(TILE, F32)]
            for x in range(16):
                total = weighted[x + 1, planes, :]
                if x % 4 == 0:
                    total = total + weighted[x, planes, :]
                if x % 4 == 3:
                    total = total + weighted[x + 2, planes, :]
                row_sum[x, planes, :] = total
                packed[0] = jnp.where(lane == x, pltpu.roll(total, x, 1), packed[0])
                packed[1] = jnp.where(lane == x, pltpu.roll(total, x + 1, 1), packed[1])
            for side in range(2):
                column_pay[side, planes, :] = packed[side]
            return carry

        lax.fori_loop(0, 6, group, 0)

    def sum_columns(column_in, store):
        def group(g, carry):
            planes = pl.ds(pl.multiple_of(g * 8, 8), 8)
            left, right = column_in[0, planes, :], column_in[1, planes, :]
            for x in range(16):
                v = row_sum[x, planes, :]
                before = jnp.where(
                    lane == 0, pltpu.roll(left, (128 - x) % 128, 1), pltpu.roll(v, 1, 1)
                )
                after = jnp.where(
                    lane == 127, pltpu.roll(right, 127 - x, 1), pltpu.roll(v, 127, 1)
                )
                total = v + jnp.where(first_y, before, 0.0) + jnp.where(last_y, after, 0.0)
                store(g, x, total * jnp.broadcast_to(inverse_ref[x : x + 1, :], TILE))
            return carry

        lax.fori_loop(0, 6, group, 0)

    for copy in row_copies:
        copy.wait_recv()
    sum_rows(weighted_1, column_pay_1)
    column_copies = [
        send_near(column_pay_1.at[0], column_in_1.at[1], 2, 18),
        send_near(column_pay_1.at[1], column_in_1.at[0], 3, 19),
    ]

    for copy in margin_copies:
        copy.wait_recv()

    def widen(own, inbox):
        centre = [own[0:8], own[8:16], inbox(1)[0:8], inbox(0)[0:8]]
        right = [inbox(3)[0:8], inbox(3)[8:16], inbox(7)[0:8], inbox(5)[0:8]]
        left = [inbox(2)[0:8], inbox(2)[8:16], inbox(6)[0:8], inbox(4)[0:8]]
        return centre + [jnp.where(lane < 64, r, l) for r, l in zip(right, left)]

    def copy_sum(tiles):
        summed = []
        for side in range(2):
            part = tiles[4 * side : 4 * side + 4]
            prev = [pltpu.roll(v, 1, 0) for v in part]
            succ = [pltpu.roll(v, 7, 0) for v in part]
            for i in range(4):
                before = jnp.where(sub == 0, prev[i - 1], prev[i])
                after = jnp.where(sub == 7, succ[(i + 1) % 4], succ[i])
                summed.append(
                    part[i] + jnp.where(first_x, before, 0.0) + jnp.where(last_x, after, 0.0)
                )
        prev = [pltpu.roll(v, 1, 1) for v in summed]
        succ = [pltpu.roll(v, 127, 1) for v in summed]
        result = []
        for i in range(8):
            other = (i + 4) % 8
            before = jnp.where(lane == 0, prev[other], prev[i])
            after = jnp.where(lane == 127, succ[other], succ[i])
            result.append(
                summed[i] + jnp.where(first_y, before, 0.0) + jnp.where(last_y, after, 0.0)
            )
        return result

    taps_x = [(s, tap_table(x_pos, s)) for s in shifts]
    centre_x = tap_table(x_pos, 0)

    def without_surface(v, wind_x, wind_y):
        slope_x = centre_x * v
        for s, tap in taps_x:
            slope_x = slope_x + tap * pltpu.roll(v, (-s) % 8, 0)
        return v - F32(TIME_STEP) * (wind_x * slope_x + wind_y * slope_y(v)) - F32(RELAX) * v

    wide = [
        widen(margin_pay[q], lambda d, q=q: margin_in[d, q]) for q in range(4)
    ]
    wide_mass = [gll_weight * v for v in wide[3]]
    wide_inverse = [1.0 / v for v in copy_sum(wide_mass)]
    for i in range(8):
        base_ref[i] = without_surface(wide[0][i], wide[1][i], wide[2][i])
        wide_ref[0, i] = wide[1][i]
        wide_ref[1, i] = wide[2][i]
        wide_ref[2, i] = wide_mass[i]
        wide_ref[3, i] = wide_inverse[i]
    for half in range(2):
        inverse_ref[8 * half : 8 * half + 8, :] = wide_inverse[half]

    for copy in column_copies:
        copy.wait_recv()

    def keep(g, x, v):
        field_1[x, pl.ds(pl.multiple_of(g * 8, 8), 8), :] = v

    sum_columns(column_in_1, keep)
    advance(lambda g, x: field_1[x, pl.ds(pl.multiple_of(g * 8, 8), 8), :], weighted_2)
    row_copies = [
        send_near(weighted_2.at[1], weighted_2.at[17], 0, 20),
        send_near(weighted_2.at[16], weighted_2.at[0], 1, 21),
    ]

    build_hot(cols_ref, hot_cols)
    for copy in rim_copies:
        copy.wait_recv()
    ocean(0, 2)
    for copy in row_copies:
        copy.wait_recv()
    sum_rows(weighted_2, column_pay_2)
    column_copies = [
        send_near(column_pay_2.at[0], column_in_2.at[1], 2, 22),
        send_near(column_pay_2.at[1], column_in_2.at[0], 3, 23),
    ]
    ocean(2, 4)

    await_all(heat_in, all_recv.at[0])
    build_left(
        rows_ref,
        lambda base: (heat_in[pl.ds(base, 8), 0, :], heat_in[pl.ds(base, 8), 1, :]),
        left_ref,
    )
    heat, frac = scatter_sums(left_ref, hot_rows, 2)
    surf_pay[...] = (heat + land_ref[...] * air_ref[0:16, :]) / (frac + land_ref[...])
    for d in range(8):
        low, high = MARGIN_ROWS[DIRECTIONS[d][0]]
        surf_copies.append(
            send_near(
                surf_pay.at[low:high, :],
                surf_in.at[REVERSE[d], 0 : high - low, :],
                d,
                8 + d,
            )
        )

    for copy in column_copies:
        copy.wait_recv()

    def put_out(g, x, v):
        air_out[pl.ds(g * 128 + x, 8, stride=16), :] = v

    sum_columns(column_in_2, put_out)
    ocean(4, 7)

    for copy in surf_copies:
        copy.wait_recv()
    surf = widen(surf_pay[...], lambda d: surf_in[d])
    moved = [
        wide_ref[2, i] * (base_ref[i] + F32(RELAX) * surf[i]) for i in range(8)
    ]
    field = [v * wide_ref[3, i] for i, v in enumerate(copy_sum(moved))]
    moved = [
        wide_ref[2, i]
        * (without_surface(field[i], wide_ref[0, i], wide_ref[1, i]) + F32(RELAX) * surf[i])
        for i in range(8)
    ]
    final = [v * wide_ref[3, i] for i, v in enumerate(copy_sum(moved)[0:2])]
    flux = [
        jnp.broadcast_to((final[h // 8] - surf[h // 8])[h % 8 : h % 8 + 1], TILE)
        for h in range(16)
    ]
    for i in range(n_blk // 8):
        idx = rows_ref[8 * i : 8 * i + 8, :]
        flux_pay[8 * i : 8 * i + 8, 0, :] = lane_gather(
            flux, lax.shift_right_logical(idx, 7), lax.bitwise_and(idx, 127)
        )
    exchange(flux_pay, flux_in, 1)
    flux_in[blk] = flux_pay[blk]

    for half in range(2):
        air_out[8 * half : 8 * half + 8, :] = final[half]
    ocean(7, 16)

    await_all(flux_in, all_recv.at[1])
    build_left(
        cols_ref,
        lambda base: (weight_ref[pl.ds(base, 8), :] * flux_in[pl.ds(base, 8), 0, :],),
        left_ref,
    )
    (inflow,) = scatter_sums(left_ref, hot_cols, 1)
    gain = F32(FLUX_GAIN) * inflow / area_ref[...]
    for h in range(16):
        here = slice(128 * h, 128 * h + 128)
        ocean_out[0:1, here] = ocean_out[0:1, here] + gain[h : h + 1]

    for copy in started:
        copy.wait_send()
    await_all(heat_pay, all_send.at[0])
    await_all(flux_pay, all_send.at[1])


def solution(mesh):
    n_face, n_blk = mesh.shape["face"], mesh.shape["blk"]

    def body(
        air_state,
        air_wind,
        jacobian,
        land_area,
        xgrid_rows,
        tracers,
        edge_coef,
        neighbours,
        vert_rate,
        ocean_area,
        send_list,
        xgrid_cols,
        xgrid_weights,
    ):
        air_shape, ocean_shape = air_state.shape, tracers.shape
        vmem = pltpu.VMEM
        air, ocean = pl.pallas_call(
            lambda *refs: interval_kernel(n_face, n_blk, *refs),
            out_shape=(vmem((768, 128), F32), vmem((32, 2048), F32)),
            in_specs=[pl.BlockSpec(memory_space=pl.ANY)] * 13,
            out_specs=(pl.BlockSpec(memory_space=vmem),) * 2,
            scratch_shapes=[
                vmem((768, 128), F32),
                vmem((512, 128), F32),
                vmem((16, 128), F32),
                vmem((16, 128), F32),
                vmem((n_blk, 128), jnp.int32),
                vmem((32, 2048), F32),
                vmem((6, 2048), F32),
                vmem((6, 2048), jnp.int32),
                vmem((16, 128), F32),
                vmem((16, 128), F32),
                vmem((2, 128), jnp.int32),
                vmem((n_blk, 128), jnp.int32),
                vmem((n_blk, 128), F32),
                pltpu.SemaphoreType.DMA((13,)),
                vmem((n_blk, 2, 128), F32),
                vmem((n_blk, 2, 128), F32),
                vmem((n_blk, 1, 128), F32),
                vmem((n_blk, 1, 128), F32),
                vmem((2, 32, 128), F32),
                vmem((2, 32, 128), F32),
                vmem((4, 16, 128), F32),
                vmem((8, 4, 16, 128), F32),
                vmem((16, 128), F32),
                vmem((8, 16, 128), F32),
                vmem((18, 48, 128), F32),
                vmem((18, 48, 128), F32),
                vmem((16, 48, 128), F32),
                vmem((2, 48, 128), F32),
                vmem((2, 48, 128), F32),
                vmem((2, 48, 128), F32),
                vmem((2, 48, 128), F32),
                vmem((16, 48, 128), F32),
                vmem((16, 128), F32),
                vmem((16, 128), F32),
                vmem((128, 128 * n_blk), BF16),
                vmem((128, 128 * n_blk), BF16),
                vmem((96, 128 * n_blk), BF16),
                vmem((8, 8, 128), F32),
                vmem((4, 8, 8, 128), F32),
                pltpu.SemaphoreType.DMA((2,)),
                pltpu.SemaphoreType.DMA((2,)),
                pltpu.SemaphoreType.DMA((26,)),
                pltpu.SemaphoreType.DMA((26,)),
            ],
            compiler_params=pltpu.CompilerParams(collective_id=0, has_side_effects=True),
            name="interval",
        )(
            air_state.reshape(768, 128),
            air_wind.reshape(512, 128),
            jacobian,
            land_area,
            xgrid_rows[0],
            tracers.reshape(32, 2048),
            edge_coef,
            neighbours,
            vert_rate.reshape(16, 128),
            ocean_area.reshape(16, 128),
            send_list.reshape(2, 128),
            xgrid_cols[0],
            xgrid_weights[0],
        )
        return air.reshape(air_shape), ocean.reshape(ocean_shape)

    both = ("face", "blk")
    in_specs = (
        P(None, None, "face", "blk"),
        P(None, None, "face", "blk"),
        P("face", "blk"),
        P("face", "blk"),
        P(both, None, None),
        P(None, None, both),
        P(None, both),
        P(None, both),
        P(both),
        P(both),
        P(both, None),
        P(both, None, None),
        P(both, None, None),
    )
    out_specs = (P(None, None, "face", "blk"), P(None, None, both))
    return jax.shard_map(body, mesh=mesh, in_specs=in_specs, out_specs=out_specs, check_vma=False)
```

```python
import jax
import jax.numpy as jnp
from jax import lax
from jax.experimental import pallas as pl
from jax.experimental.pallas import tpu as pltpu
from jax.sharding import PartitionSpec as P

GLL = 4
DERIV = (
    (-3.0, 4.045084971874737, -1.545084971874737, 0.5),
    (-0.8090169943749475, 0.0, 1.118033988749895, -0.30901699437494745),
    (0.30901699437494745, -1.118033988749895, 0.0, 0.8090169943749475),
    (-0.5, 1.545084971874737, -4.045084971874737, 3.0),
)
TIME_STEP = 0.05
RELAX = 0.3
FLUX_GAIN = 0.2
DIRECTIONS = ((-1, 0), (1, 0), (0, -1), (0, 1), (-1, -1), (-1, 1), (1, -1), (1, 1))
REVERSE = (1, 0, 3, 2, 7, 6, 5, 4)
MARGIN_ROWS = {-1: (0, 8), 1: (8, 16), 0: (0, 16)}
MESH = pl.DeviceIdType.MESH
F32 = jnp.float32
BF16 = jnp.bfloat16
TILE = (8, 128)
PARTS = 2


def lane_gather(rows, hi, lo):
    found = jnp.zeros(TILE, F32)
    for h, row in enumerate(rows):
        found = jnp.where(hi == h, jnp.take_along_axis(row, lo, axis=1), found)
    return found


def tap_table(position, shift):
    table = jnp.zeros(TILE, F32)
    for i in range(GLL):
        if 0 <= i + shift < GLL:
            table = jnp.where(position == i, F32(DERIV[i][i + shift]), table)
    return table


def build_hot(idx_ref, hot_ref):
    rows = lax.broadcasted_iota(jnp.int32, (128, 128), 0)

    def step(r8, carry):
        base = pl.multiple_of(r8 * 8, 8)
        for i in range(8):
            lo = lax.bitwise_and(idx_ref[pl.ds(base + i, 1), :], 127)
            hot = jnp.where(rows == jnp.broadcast_to(lo, (128, 128)), 1.0, 0.0).astype(BF16)
            hot_ref[:, pl.ds(pl.multiple_of((base + i) * 128, 128), 128)] = hot
        return carry

    lax.fori_loop(0, idx_ref.shape[0] // 8, step, 0)


def build_left(idx_ref, values_at, left_ref):
    rows = lax.broadcasted_iota(jnp.int32, (16, 128), 0)

    def step(r8, carry):
        base = pl.multiple_of(r8 * 8, 8)
        hi = lax.shift_right_logical(idx_ref[pl.ds(base, 8), :], 7)
        parts = []
        for rest in values_at(base):
            for _ in range(PARTS):
                part = rest.astype(BF16).astype(F32)
                parts.append(part)
                rest = rest - part
        for i in range(8):
            mine = jnp.broadcast_to(hi[i : i + 1], (16, 128)) == rows
            left = [
                jnp.where(mine, jnp.broadcast_to(p[i : i + 1], (16, 128)), 0.0).astype(BF16)
                for p in parts
            ]
            left_ref[0 : 16 * len(parts), pl.ds(pl.multiple_of((base + i) * 128, 128), 128)] = (
                jnp.concatenate(left, axis=0)
            )
        return carry

    lax.fori_loop(0, idx_ref.shape[0] // 8, step, 0)


def scatter_sums(left_ref, hot_ref, count):
    size = 16 * PARTS
    total = lax.dot_general(
        left_ref[0 : size * count, :],
        hot_ref[...],
        (((1,), (1,)), ((), ())),
        preferred_element_type=F32,
    )
    return [
        sum(total[size * q + 16 * p : size * q + 16 * p + 16] for p in range(PARTS))
        for q in range(count)
    ]


def interval_kernel(
    n_face,
    n_blk,
    air_hbm,
    wind_hbm,
    jac_hbm,
    land_hbm,
    rows_hbm,
    tracer_hbm,
    coef_hbm,
    near_hbm,
    vert_hbm,
    area_hbm,
    send_hbm,
    cols_hbm,
    weight_hbm,
    air_out,
    ocean_out,
    air_ref,
    wind_ref,
    jac_ref,
    land_ref,
    rows_ref,
    tracer_ref,
    coef_ref,
    near_ref,
    vert_ref,
    area_ref,
    send_ref,
    cols_ref,
    weight_ref,
    load_sem,
    heat_pay,
    heat_in,
    flux_pay,
    flux_in,
    rim_pay,
    rim_in,
    margin_pay,
    margin_in,
    surf_pay,
    surf_in,
    weighted_1,
    weighted_2,
    row_sum,
    column_pay_1,
    column_in_1,
    column_pay_2,
    column_in_2,
    field_1,
    mass_ref,
    inverse_ref,
    hot_rows,
    hot_cols,
    left_ref,
    base_ref,
    wide_ref,
    all_send,
    all_recv,
    near_send,
    near_recv,
):
    face, blk = lax.axis_index("face"), lax.axis_index("blk")

    def step_to(d):
        df, db = DIRECTIONS[d]
        return (lax.rem(face + df + n_face, n_face), lax.rem(blk + db + n_blk, n_blk))

    names = (
        *("cols", "weight", "tracer", "send", "air", "wind", "jac"),
        *("rows", "land", "coef", "near", "vert", "area"),
    )
    pairs = {
        "air": (air_hbm, air_ref),
        "wind": (wind_hbm, wind_ref),
        "jac": (jac_hbm, jac_ref),
        "land": (land_hbm, land_ref),
        "rows": (rows_hbm, rows_ref),
        "tracer": (tracer_hbm, tracer_ref),
        "coef": (coef_hbm, coef_ref),
        "near": (near_hbm, near_ref),
        "vert": (vert_hbm, vert_ref),
        "area": (area_hbm, area_ref),
        "send": (send_hbm, send_ref),
        "cols": (cols_hbm, cols_ref),
        "weight": (weight_hbm, weight_ref),
    }
    loads = {
        name: pltpu.make_async_copy(*pairs[name], load_sem.at[i]) for i, name in enumerate(names)
    }
    for name in names:
        loads[name].start()

    def loaded(*wanted):
        for name in wanted:
            loads[name].wait()

    def every_peer(act):
        half = n_blk // 2
        act(lax.rem(blk + half, n_blk))

        def both(k, carry):
            act(lax.rem(blk + half + k, n_blk))
            act(lax.rem(blk + half - k, n_blk))
            return carry

        lax.fori_loop(1, half, both, 0)

    barrier = pltpu.get_barrier_semaphore()
    for d in (4, 5, 6, 7, 0, 1):
        pl.semaphore_signal(barrier, inc=1, device_id=step_to(d), device_id_type=MESH)
    every_peer(
        lambda peer: pl.semaphore_signal(
            barrier, inc=1, device_id=(face, peer), device_id_type=MESH
        )
    )

    sub = lax.broadcasted_iota(jnp.int32, TILE, 0)
    lane = lax.broadcasted_iota(jnp.int32, TILE, 1)
    x_pos, y_pos = lax.bitwise_and(sub, 3), lax.bitwise_and(lane, 3)
    first_x, last_x = x_pos == 0, x_pos == 3
    first_y, last_y = y_pos == 0, y_pos == 3
    sixth, five_sixths = F32(1.0 / 6.0), F32(5.0 / 6.0)
    gll_weight = jnp.where(first_x | last_x, sixth, five_sixths) * jnp.where(
        first_y | last_y, sixth, five_sixths
    )
    shifts = (-3, -2, -1, 1, 2, 3)

    loaded("cols", "weight", "tracer")
    surface = [
        jnp.broadcast_to(tracer_ref[0:1, 128 * h : 128 * h + 128], TILE) for h in range(16)
    ]
    for i in range(n_blk // 8):
        idx = cols_ref[8 * i : 8 * i + 8, :]
        weight = weight_ref[8 * i : 8 * i + 8, :]
        at = lane_gather(surface, lax.shift_right_logical(idx, 7), lax.bitwise_and(idx, 127))
        heat_pay[8 * i : 8 * i + 8, 0, :] = weight * at
        heat_pay[8 * i : 8 * i + 8, 1, :] = weight

    pl.semaphore_wait(barrier, n_blk - 1 + 6)

    def exchange(pay, inbox, slot):
        every_peer(
            lambda peer: pltpu.make_async_remote_copy(
                src_ref=pay.at[peer],
                dst_ref=inbox.at[blk],
                send_sem=all_send.at[slot],
                recv_sem=all_recv.at[slot],
                device_id=(face, peer),
                device_id_type=MESH,
            ).start()
        )

    def await_all(ref, sem):
        rest = ref.at[pl.ds(0, n_blk - 1)]
        pltpu.make_async_copy(rest, rest, sem).wait()

    started = []

    def send_near(src, dst, d, slot):
        copy = pltpu.make_async_remote_copy(
            src_ref=src,
            dst_ref=dst,
            send_sem=near_send.at[slot],
            recv_sem=near_recv.at[slot],
            device_id=step_to(d),
            device_id_type=MESH,
        )
        copy.start()
        started.append(copy)
        return copy

    exchange(heat_pay, heat_in, 0)
    heat_in[blk] = heat_pay[blk]

    loaded("air", "wind", "jac")
    margin_pay[0] = air_ref[0:16, :]
    margin_pay[1] = wind_ref[0:16, :]
    margin_pay[2] = wind_ref[256:272, :]
    margin_pay[3] = jac_ref[...]
    for half in range(2):
        mass_ref[8 * half : 8 * half + 8, :] = gll_weight * jac_ref[8 * half : 8 * half + 8, :]

    margin_copies, surf_copies = [], []
    for d in range(8):
        low, high = MARGIN_ROWS[DIRECTIONS[d][0]]
        margin_copies.append(
            send_near(
                margin_pay.at[:, low:high, :],
                margin_in.at[REVERSE[d], :, 0 : high - low, :],
                d,
                d,
            )
        )

    loaded("send")
    for side in range(2):
        idx = jnp.broadcast_to(send_ref[side : side + 1, :], TILE)
        hi, lo = lax.shift_right_logical(idx, 7), lax.bitwise_and(idx, 127)
        for g in range(4):
            tiles = [tracer_ref[8 * g : 8 * g + 8, 128 * h : 128 * h + 128] for h in range(16)]
            rim_pay[side, 8 * g : 8 * g + 8, :] = lane_gather(tiles, hi, lo)

    rim_copies = [
        send_near(rim_pay.at[0], rim_in.at[1], 2, 24),
        send_near(rim_pay.at[1], rim_in.at[0], 3, 25),
    ]

    taps_y = [(s, tap_table(y_pos, s)) for s in shifts]
    centre_y = tap_table(y_pos, 0)

    def slope_y(v):
        total = centre_y * v
        for s, tap in taps_y:
            total = total + tap * pltpu.roll(v, (-s) % 128, 1)
        return total

    def advance(field_at, target):
        def group(g, carry):
            half = lax.rem(g, 2) * 128
            planes = pl.ds(pl.multiple_of(g * 8, 8), 8)
            for e in range(4):
                fields = [field_at(g, 4 * e + k) for k in range(4)]
                for i in range(4):
                    x = 4 * e + i
                    slope_x = None
                    for k in range(4):
                        if DERIV[i][k]:
                            term = F32(DERIV[i][k]) * fields[k]
                            slope_x = term if slope_x is None else slope_x + term
                    wind_x = wind_ref[pl.ds(half + x, 8, stride=16), :]
                    wind_y = wind_ref[pl.ds(half + 256 + x, 8, stride=16), :]
                    tendency = wind_x * slope_x + wind_y * slope_y(fields[i])
                    moved = fields[i] - F32(TIME_STEP) * tendency
                    mass = jnp.broadcast_to(mass_ref[x : x + 1, :], TILE)
                    target[x + 1, planes, :] = mass * moved
            return carry

        lax.fori_loop(0, 6, group, 0)

    advance(lambda g, x: air_ref[pl.ds(g * 128 + x, 8, stride=16), :], weighted_1)
    row_copies = [
        send_near(weighted_1.at[1], weighted_1.at[17], 0, 16),
        send_near(weighted_1.at[16], weighted_1.at[0], 1, 17),
    ]
    loaded("rows", "land", "coef", "near", "vert", "area")
    build_hot(rows_ref, hot_rows)

    def ocean(first, last):
        def block(j, carry):
            here = pl.ds(pl.multiple_of(j * 128, 128), 128)
            own = [tracer_ref[8 * g : 8 * g + 8, here] for g in range(4)]
            lateral = [jnp.zeros(TILE, F32) for g in range(4)]
            for e in range(6):
                idx = jnp.broadcast_to(near_ref[e : e + 1, here], TILE)
                coef = jnp.broadcast_to(coef_ref[e : e + 1, here], TILE)
                hi, lo = lax.shift_right_logical(idx, 7), lax.bitwise_and(idx, 127)
                found = [jnp.zeros(TILE, F32) for g in range(4)]
                for h in range(18):
                    mine = hi == h
                    for g in range(4):
                        if h < 16:
                            tile = tracer_ref[8 * g : 8 * g + 8, 128 * h : 128 * h + 128]
                        else:
                            tile = rim_in[h - 16, 8 * g : 8 * g + 8, :]
                        found[g] = jnp.where(mine, jnp.take_along_axis(tile, lo, axis=1), found[g])
                for g in range(4):
                    lateral[g] = lateral[g] + coef * (found[g] - own[g])
            rate = jnp.broadcast_to(vert_ref[pl.ds(j, 1), :], TILE)
            for t in range(2):
                top, low = own[2 * t], own[2 * t + 1]
                down = [pltpu.roll(v, 1, 0) for v in (top, low)]
                up = [pltpu.roll(v, 7, 0) for v in (top, low)]
                above = [jnp.where(sub == 0, top, down[0]), jnp.where(sub == 0, down[0], down[1])]
                below = [jnp.where(sub == 7, up[1], up[0]), jnp.where(sub == 7, low, up[1])]
                for i, v in enumerate((top, low)):
                    g = 2 * t + i
                    vertical = rate * ((above[i] - v) + (below[i] - v))
                    ocean_out[8 * g : 8 * g + 8, here] = v + lateral[g] + vertical
            return carry

        lax.fori_loop(first, last, block, 0)

    def sum_rows(weighted, column_pay):
        def group(g, carry):
            planes = pl.ds(pl.multiple_of(g * 8, 8), 8)
            packed = [jnp.zeros(TILE, F32), jnp.zeros(TILE, F32)]
            for x in range(16):
                total = weighted[x + 1, planes, :]
                if x % 4 == 0:
                    total = total + weighted[x, planes, :]
                if x % 4 == 3:
                    total = total + weighted[x + 2, planes, :]
                row_sum[x, planes, :] = total
                packed[0] = jnp.where(lane == x, pltpu.roll(total, x, 1), packed[0])
                packed[1] = jnp.where(lane == x, pltpu.roll(total, x + 1, 1), packed[1])
            for side in range(2):
                column_pay[side, planes, :] = packed[side]
            return carry

        lax.fori_loop(0, 6, group, 0)

    def sum_columns(column_in, store):
        def group(g, carry):
            planes = pl.ds(pl.multiple_of(g * 8, 8), 8)
            left, right = column_in[0, planes, :], column_in[1, planes, :]
            for x in range(16):
                v = row_sum[x, planes, :]
                before = jnp.where(
                    lane == 0, pltpu.roll(left, (128 - x) % 128, 1), pltpu.roll(v, 1, 1)
                )
                after = jnp.where(
                    lane == 127, pltpu.roll(right, 127 - x, 1), pltpu.roll(v, 127, 1)
                )
                total = v + jnp.where(first_y, before, 0.0) + jnp.where(last_y, after, 0.0)
                store(g, x, total * jnp.broadcast_to(inverse_ref[x : x + 1, :], TILE))
            return carry

        lax.fori_loop(0, 6, group, 0)

    for copy in rim_copies:
        copy.wait_recv()
    ocean(0, 3)
    for copy in row_copies:
        copy.wait_recv()
    sum_rows(weighted_1, column_pay_1)
    column_copies = [
        send_near(column_pay_1.at[0], column_in_1.at[1], 2, 18),
        send_near(column_pay_1.at[1], column_in_1.at[0], 3, 19),
    ]

    for copy in margin_copies:
        copy.wait_recv()

    def widen(own, inbox):
        centre = [own[0:8], own[8:16], inbox(1)[0:8], inbox(0)[0:8]]
        right = [inbox(3)[0:8], inbox(3)[8:16], inbox(7)[0:8], inbox(5)[0:8]]
        left = [inbox(2)[0:8], inbox(2)[8:16], inbox(6)[0:8], inbox(4)[0:8]]
        return centre + [jnp.where(lane < 64, r, l) for r, l in zip(right, left)]

    def copy_sum(tiles):
        summed = []
        for side in range(2):
            part = tiles[4 * side : 4 * side + 4]
            prev = [pltpu.roll(v, 1, 0) for v in part]
            succ = [pltpu.roll(v, 7, 0) for v in part]
            for i in range(4):
                before = jnp.where(sub == 0, prev[i - 1], prev[i])
                after = jnp.where(sub == 7, succ[(i + 1) % 4], succ[i])
                summed.append(
                    part[i] + jnp.where(first_x, before, 0.0) + jnp.where(last_x, after, 0.0)
                )
        prev = [pltpu.roll(v, 1, 1) for v in summed]
        succ = [pltpu.roll(v, 127, 1) for v in summed]
        result = []
        for i in range(8):
            other = (i + 4) % 8
            before = jnp.where(lane == 0, prev[other], prev[i])
            after = jnp.where(lane == 127, succ[other], succ[i])
            result.append(
                summed[i] + jnp.where(first_y, before, 0.0) + jnp.where(last_y, after, 0.0)
            )
        return result

    taps_x = [(s, tap_table(x_pos, s)) for s in shifts]
    centre_x = tap_table(x_pos, 0)

    def without_surface(v, wind_x, wind_y):
        slope_x = centre_x * v
        for s, tap in taps_x:
            slope_x = slope_x + tap * pltpu.roll(v, (-s) % 8, 0)
        return v - F32(TIME_STEP) * (wind_x * slope_x + wind_y * slope_y(v)) - F32(RELAX) * v

    wide = [
        widen(margin_pay[q], lambda d, q=q: margin_in[d, q]) for q in range(4)
    ]
    wide_mass = [gll_weight * v for v in wide[3]]
    wide_inverse = [1.0 / v for v in copy_sum(wide_mass)]
    for i in range(8):
        base_ref[i] = without_surface(wide[0][i], wide[1][i], wide[2][i])
        wide_ref[0, i] = wide[1][i]
        wide_ref[1, i] = wide[2][i]
        wide_ref[2, i] = wide_mass[i]
        wide_ref[3, i] = wide_inverse[i]
    for half in range(2):
        inverse_ref[8 * half : 8 * half + 8, :] = wide_inverse[half]

    ocean(3, 6)
    for copy in column_copies:
        copy.wait_recv()

    def keep(g, x, v):
        field_1[x, pl.ds(pl.multiple_of(g * 8, 8), 8), :] = v

    sum_columns(column_in_1, keep)
    advance(lambda g, x: field_1[x, pl.ds(pl.multiple_of(g * 8, 8), 8), :], weighted_2)
    row_copies = [
        send_near(weighted_2.at[1], weighted_2.at[17], 0, 20),
        send_near(weighted_2.at[16], weighted_2.at[0], 1, 21),
    ]

    build_hot(cols_ref, hot_cols)

    await_all(heat_in, all_recv.at[0])
    build_left(
        rows_ref,
        lambda base: (heat_in[pl.ds(base, 8), 0, :], heat_in[pl.ds(base, 8), 1, :]),
        left_ref,
    )
    heat, frac = scatter_sums(left_ref, hot_rows, 2)
    surf_pay[...] = (heat + land_ref[...] * air_ref[0:16, :]) / (frac + land_ref[...])
    for d in range(8):
        low, high = MARGIN_ROWS[DIRECTIONS[d][0]]
        surf_copies.append(
            send_near(
                surf_pay.at[low:high, :],
                surf_in.at[REVERSE[d], 0 : high - low, :],
                d,
                8 + d,
            )
        )

    for copy in row_copies:
        copy.wait_recv()
    sum_rows(weighted_2, column_pay_2)
    column_copies = [
        send_near(column_pay_2.at[0], column_in_2.at[1], 2, 22),
        send_near(column_pay_2.at[1], column_in_2.at[0], 3, 23),
    ]
    ocean(6, 9)

    for copy in surf_copies:
        copy.wait_recv()
    surf = widen(surf_pay[...], lambda d: surf_in[d])
    moved = [
        wide_ref[2, i] * (base_ref[i] + F32(RELAX) * surf[i]) for i in range(8)
    ]
    field = [v * wide_ref[3, i] for i, v in enumerate(copy_sum(moved))]
    moved = [
        wide_ref[2, i]
        * (without_surface(field[i], wide_ref[0, i], wide_ref[1, i]) + F32(RELAX) * surf[i])
        for i in range(8)
    ]
    final = [v * wide_ref[3, i] for i, v in enumerate(copy_sum(moved)[0:2])]
    flux = [
        jnp.broadcast_to((final[h // 8] - surf[h // 8])[h % 8 : h % 8 + 1], TILE)
        for h in range(16)
    ]
    for i in range(n_blk // 8):
        idx = rows_ref[8 * i : 8 * i + 8, :]
        flux_pay[8 * i : 8 * i + 8, 0, :] = lane_gather(
            flux, lax.shift_right_logical(idx, 7), lax.bitwise_and(idx, 127)
        )
    exchange(flux_pay, flux_in, 1)
    flux_in[blk] = flux_pay[blk]

    for copy in column_copies:
        copy.wait_recv()

    def put_out(g, x, v):
        air_out[pl.ds(g * 128 + x, 8, stride=16), :] = v

    sum_columns(column_in_2, put_out)
    for half in range(2):
        air_out[8 * half : 8 * half + 8, :] = final[half]
    ocean(9, 16)

    await_all(flux_in, all_recv.at[1])
    build_left(
        cols_ref,
        lambda base: (weight_ref[pl.ds(base, 8), :] * flux_in[pl.ds(base, 8), 0, :],),
        left_ref,
    )
    (inflow,) = scatter_sums(left_ref, hot_cols, 1)
    gain = F32(FLUX_GAIN) * inflow / area_ref[...]
    for h in range(16):
        here = slice(128 * h, 128 * h + 128)
        ocean_out[0:1, here] = ocean_out[0:1, here] + gain[h : h + 1]

    for copy in started:
        copy.wait_send()
    await_all(heat_pay, all_send.at[0])
    await_all(flux_pay, all_send.at[1])


def solution(mesh):
    n_face, n_blk = mesh.shape["face"], mesh.shape["blk"]

    def body(
        air_state,
        air_wind,
        jacobian,
        land_area,
        xgrid_rows,
        tracers,
        edge_coef,
        neighbours,
        vert_rate,
        ocean_area,
        send_list,
        xgrid_cols,
        xgrid_weights,
    ):
        air_shape, ocean_shape = air_state.shape, tracers.shape
        vmem = pltpu.VMEM
        air, ocean = pl.pallas_call(
            lambda *refs: interval_kernel(n_face, n_blk, *refs),
            out_shape=(vmem((768, 128), F32), vmem((32, 2048), F32)),
            in_specs=[pl.BlockSpec(memory_space=pl.ANY)] * 13,
            out_specs=(pl.BlockSpec(memory_space=vmem),) * 2,
            scratch_shapes=[
                vmem((768, 128), F32),
                vmem((512, 128), F32),
                vmem((16, 128), F32),
                vmem((16, 128), F32),
                vmem((n_blk, 128), jnp.int32),
                vmem((32, 2048), F32),
                vmem((6, 2048), F32),
                vmem((6, 2048), jnp.int32),
                vmem((16, 128), F32),
                vmem((16, 128), F32),
                vmem((2, 128), jnp.int32),
                vmem((n_blk, 128), jnp.int32),
                vmem((n_blk, 128), F32),
                pltpu.SemaphoreType.DMA((13,)),
                vmem((n_blk, 2, 128), F32),
                vmem((n_blk, 2, 128), F32),
                vmem((n_blk, 1, 128), F32),
                vmem((n_blk, 1, 128), F32),
                vmem((2, 32, 128), F32),
                vmem((2, 32, 128), F32),
                vmem((4, 16, 128), F32),
                vmem((8, 4, 16, 128), F32),
                vmem((16, 128), F32),
                vmem((8, 16, 128), F32),
                vmem((18, 48, 128), F32),
                vmem((18, 48, 128), F32),
                vmem((16, 48, 128), F32),
                vmem((2, 48, 128), F32),
                vmem((2, 48, 128), F32),
                vmem((2, 48, 128), F32),
                vmem((2, 48, 128), F32),
                vmem((16, 48, 128), F32),
                vmem((16, 128), F32),
                vmem((16, 128), F32),
                vmem((128, 128 * n_blk), BF16),
                vmem((128, 128 * n_blk), BF16),
                vmem((32 * PARTS, 128 * n_blk), BF16),
                vmem((8, 8, 128), F32),
                vmem((4, 8, 8, 128), F32),
                pltpu.SemaphoreType.DMA((2,)),
                pltpu.SemaphoreType.DMA((2,)),
                pltpu.SemaphoreType.DMA((26,)),
                pltpu.SemaphoreType.DMA((26,)),
            ],
            compiler_params=pltpu.CompilerParams(collective_id=0, has_side_effects=True),
            name="interval",
        )(
            air_state.reshape(768, 128),
            air_wind.reshape(512, 128),
            jacobian,
            land_area,
            xgrid_rows[0],
            tracers.reshape(32, 2048),
            edge_coef,
            neighbours,
            vert_rate.reshape(16, 128),
            ocean_area.reshape(16, 128),
            send_list.reshape(2, 128),
            xgrid_cols[0],
            xgrid_weights[0],
        )
        return air.reshape(air_shape), ocean.reshape(ocean_shape)

    both = ("face", "blk")
    in_specs = (
        P(None, None, "face", "blk"),
        P(None, None, "face", "blk"),
        P("face", "blk"),
        P("face", "blk"),
        P(both, None, None),
        P(None, None, both),
        P(None, both),
        P(None, both),
        P(both),
        P(both),
        P(both, None),
        P(both, None, None),
        P(both, None, None),
    )
    out_specs = (P(None, None, "face", "blk"), P(None, None, both))
    return jax.shard_map(body, mesh=mesh, in_specs=in_specs, out_specs=out_specs, check_vma=False)
```

```python
import jax
import jax.numpy as jnp
from jax import lax
from jax.experimental import pallas as pl
from jax.experimental.pallas import tpu as pltpu
from jax.sharding import PartitionSpec as P

GLL = 4
DERIV = (
    (-3.0, 4.045084971874737, -1.545084971874737, 0.5),
    (-0.8090169943749475, 0.0, 1.118033988749895, -0.30901699437494745),
    (0.30901699437494745, -1.118033988749895, 0.0, 0.8090169943749475),
    (-0.5, 1.545084971874737, -4.045084971874737, 3.0),
)
TIME_STEP = 0.05
RELAX = 0.3
FLUX_GAIN = 0.2
DIRECTIONS = ((-1, 0), (1, 0), (0, -1), (0, 1), (-1, -1), (-1, 1), (1, -1), (1, 1))
REVERSE = (1, 0, 3, 2, 7, 6, 5, 4)
MARGIN_ROWS = {-1: (0, 8), 1: (8, 16), 0: (0, 16)}
MESH = pl.DeviceIdType.MESH
F32 = jnp.float32
BF16 = jnp.bfloat16
TILE = (8, 128)
PARTS = 2
EARLY = 5


def lane_gather(rows, hi, lo):
    found = jnp.zeros(TILE, F32)
    for h, row in enumerate(rows):
        found = jnp.where(hi == h, jnp.take_along_axis(row, lo, axis=1), found)
    return found


def tap_table(position, shift):
    table = jnp.zeros(TILE, F32)
    for i in range(GLL):
        if 0 <= i + shift < GLL:
            table = jnp.where(position == i, F32(DERIV[i][i + shift]), table)
    return table


def build_hot(idx_ref, hot_ref):
    rows = lax.broadcasted_iota(jnp.int32, (128, 128), 0)

    def step(r8, carry):
        base = pl.multiple_of(r8 * 8, 8)
        for i in range(8):
            lo = lax.bitwise_and(idx_ref[pl.ds(base + i, 1), :], 127)
            hot = jnp.where(rows == jnp.broadcast_to(lo, (128, 128)), 1.0, 0.0).astype(BF16)
            hot_ref[:, pl.ds(pl.multiple_of((base + i) * 128, 128), 128)] = hot
        return carry

    lax.fori_loop(0, idx_ref.shape[0] // 8, step, 0)


def build_left(idx_ref, values_at, left_ref):
    rows = lax.broadcasted_iota(jnp.int32, (16, 128), 0)

    def step(r8, carry):
        base = pl.multiple_of(r8 * 8, 8)
        hi = lax.shift_right_logical(idx_ref[pl.ds(base, 8), :], 7)
        parts = []
        for rest in values_at(base):
            for _ in range(PARTS):
                part = rest.astype(BF16).astype(F32)
                parts.append(part)
                rest = rest - part
        for i in range(8):
            mine = jnp.broadcast_to(hi[i : i + 1], (16, 128)) == rows
            left = [
                jnp.where(mine, jnp.broadcast_to(p[i : i + 1], (16, 128)), 0.0).astype(BF16)
                for p in parts
            ]
            left_ref[0 : 16 * len(parts), pl.ds(pl.multiple_of((base + i) * 128, 128), 128)] = (
                jnp.concatenate(left, axis=0)
            )
        return carry

    lax.fori_loop(0, idx_ref.shape[0] // 8, step, 0)


def scatter_sums(left_ref, hot_ref, count):
    size = 16 * PARTS
    total = lax.dot_general(
        left_ref[0 : size * count, :],
        hot_ref[...],
        (((1,), (1,)), ((), ())),
        preferred_element_type=F32,
    )
    return [
        sum(total[size * q + 16 * p : size * q + 16 * p + 16] for p in range(PARTS))
        for q in range(count)
    ]


def interval_kernel(
    n_face,
    n_blk,
    air_hbm,
    wind_hbm,
    jac_hbm,
    land_hbm,
    rows_hbm,
    tracer_hbm,
    coef_hbm,
    near_hbm,
    vert_hbm,
    area_hbm,
    send_hbm,
    cols_hbm,
    weight_hbm,
    air_out,
    ocean_out,
    air_ref,
    wind_ref,
    jac_ref,
    land_ref,
    rows_ref,
    tracer_ref,
    coef_ref,
    near_ref,
    vert_ref,
    area_ref,
    send_ref,
    cols_ref,
    weight_ref,
    load_sem,
    heat_pay,
    heat_in,
    flux_pay,
    flux_in,
    rim_pay,
    rim_in,
    margin_pay,
    margin_in,
    surf_pay,
    surf_in,
    weighted_1,
    weighted_2,
    row_sum,
    column_pay_1,
    column_in_1,
    column_pay_2,
    column_in_2,
    field_1,
    mass_ref,
    inverse_ref,
    hot_rows,
    hot_cols,
    left_ref,
    base_ref,
    wide_ref,
    all_send,
    all_recv,
    near_send,
    near_recv,
):
    face, blk = lax.axis_index("face"), lax.axis_index("blk")

    def step_to(d):
        df, db = DIRECTIONS[d]
        return (lax.rem(face + df + n_face, n_face), lax.rem(blk + db + n_blk, n_blk))

    names = (
        *("cols", "weight", "tracer", "send", "air", "wind", "jac"),
        *("rows", "land", "coef", "near", "vert", "area"),
    )
    pairs = {
        "air": (air_hbm, air_ref),
        "wind": (wind_hbm, wind_ref),
        "jac": (jac_hbm, jac_ref),
        "land": (land_hbm, land_ref),
        "rows": (rows_hbm, rows_ref),
        "tracer": (tracer_hbm, tracer_ref),
        "coef": (coef_hbm, coef_ref),
        "near": (near_hbm, near_ref),
        "vert": (vert_hbm, vert_ref),
        "area": (area_hbm, area_ref),
        "send": (send_hbm, send_ref),
        "cols": (cols_hbm, cols_ref),
        "weight": (weight_hbm, weight_ref),
    }
    loads = {
        name: pltpu.make_async_copy(*pairs[name], load_sem.at[i]) for i, name in enumerate(names)
    }
    for name in names:
        loads[name].start()

    def loaded(*wanted):
        for name in wanted:
            loads[name].wait()

    def every_peer(act):
        half = n_blk // 2
        act(lax.rem(blk + half, n_blk))

        def both(k, carry):
            act(lax.rem(blk + half + k, n_blk))
            act(lax.rem(blk + half - k, n_blk))
            return carry

        lax.fori_loop(1, half, both, 0)

    barrier = pltpu.get_barrier_semaphore()
    for d in (4, 5, 6, 7, 0, 1):
        pl.semaphore_signal(barrier, inc=1, device_id=step_to(d), device_id_type=MESH)
    every_peer(
        lambda peer: pl.semaphore_signal(
            barrier, inc=1, device_id=(face, peer), device_id_type=MESH
        )
    )

    sub = lax.broadcasted_iota(jnp.int32, TILE, 0)
    lane = lax.broadcasted_iota(jnp.int32, TILE, 1)
    x_pos, y_pos = lax.bitwise_and(sub, 3), lax.bitwise_and(lane, 3)
    first_x, last_x = x_pos == 0, x_pos == 3
    first_y, last_y = y_pos == 0, y_pos == 3
    sixth, five_sixths = F32(1.0 / 6.0), F32(5.0 / 6.0)
    gll_weight = jnp.where(first_x | last_x, sixth, five_sixths) * jnp.where(
        first_y | last_y, sixth, five_sixths
    )
    shifts = (-3, -2, -1, 1, 2, 3)

    loaded("cols", "weight", "tracer")
    surface = [
        jnp.broadcast_to(tracer_ref[0:1, 128 * h : 128 * h + 128], TILE) for h in range(16)
    ]
    for i in range(n_blk // 8):
        idx = cols_ref[8 * i : 8 * i + 8, :]
        weight = weight_ref[8 * i : 8 * i + 8, :]
        at = lane_gather(surface, lax.shift_right_logical(idx, 7), lax.bitwise_and(idx, 127))
        heat_pay[8 * i : 8 * i + 8, 0, :] = weight * at
        heat_pay[8 * i : 8 * i + 8, 1, :] = weight

    loaded("air", "wind", "jac")
    margin_pay[0] = air_ref[0:16, :]
    margin_pay[1] = wind_ref[0:16, :]
    margin_pay[2] = wind_ref[256:272, :]
    margin_pay[3] = jac_ref[...]
    for half in range(2):
        mass_ref[8 * half : 8 * half + 8, :] = gll_weight * jac_ref[8 * half : 8 * half + 8, :]

    loaded("send")
    for side in range(2):
        idx = jnp.broadcast_to(send_ref[side : side + 1, :], TILE)
        hi, lo = lax.shift_right_logical(idx, 7), lax.bitwise_and(idx, 127)
        for g in range(4):
            tiles = [tracer_ref[8 * g : 8 * g + 8, 128 * h : 128 * h + 128] for h in range(16)]
            rim_pay[side, 8 * g : 8 * g + 8, :] = lane_gather(tiles, hi, lo)

    taps_y = [(s, tap_table(y_pos, s)) for s in shifts]
    centre_y = tap_table(y_pos, 0)

    def slope_y(v):
        total = centre_y * v
        for s, tap in taps_y:
            total = total + tap * pltpu.roll(v, (-s) % 128, 1)
        return total

    def advance(field_at, target):
        def group(g, carry):
            half = lax.rem(g, 2) * 128
            planes = pl.ds(pl.multiple_of(g * 8, 8), 8)
            for e in range(4):
                fields = [field_at(g, 4 * e + k) for k in range(4)]
                for i in range(4):
                    x = 4 * e + i
                    slope_x = None
                    for k in range(4):
                        if DERIV[i][k]:
                            term = F32(DERIV[i][k]) * fields[k]
                            slope_x = term if slope_x is None else slope_x + term
                    wind_x = wind_ref[pl.ds(half + x, 8, stride=16), :]
                    wind_y = wind_ref[pl.ds(half + 256 + x, 8, stride=16), :]
                    tendency = wind_x * slope_x + wind_y * slope_y(fields[i])
                    moved = fields[i] - F32(TIME_STEP) * tendency
                    mass = jnp.broadcast_to(mass_ref[x : x + 1, :], TILE)
                    target[x + 1, planes, :] = mass * moved
            return carry

        lax.fori_loop(0, 6, group, 0)

    advance(lambda g, x: air_ref[pl.ds(g * 128 + x, 8, stride=16), :], weighted_1)
    loaded("rows", "land", "coef", "near", "vert", "area")
    build_hot(rows_ref, hot_rows)

    pl.semaphore_wait(barrier, n_blk - 1 + 6)

    def exchange(pay, inbox, slot):
        every_peer(
            lambda peer: pltpu.make_async_remote_copy(
                src_ref=pay.at[peer],
                dst_ref=inbox.at[blk],
                send_sem=all_send.at[slot],
                recv_sem=all_recv.at[slot],
                device_id=(face, peer),
                device_id_type=MESH,
            ).start()
        )

    def await_all(ref, sem):
        rest = ref.at[pl.ds(0, n_blk - 1)]
        pltpu.make_async_copy(rest, rest, sem).wait()

    started = []

    def send_near(src, dst, d, slot):
        copy = pltpu.make_async_remote_copy(
            src_ref=src,
            dst_ref=dst,
            send_sem=near_send.at[slot],
            recv_sem=near_recv.at[slot],
            device_id=step_to(d),
            device_id_type=MESH,
        )
        copy.start()
        started.append(copy)
        return copy

    exchange(heat_pay, heat_in, 0)
    heat_in[blk] = heat_pay[blk]

    margin_copies, surf_copies = [], []
    for d in range(8):
        low, high = MARGIN_ROWS[DIRECTIONS[d][0]]
        margin_copies.append(
            send_near(
                margin_pay.at[:, low:high, :],
                margin_in.at[REVERSE[d], :, 0 : high - low, :],
                d,
                d,
            )
        )

    rim_copies = [
        send_near(rim_pay.at[0], rim_in.at[1], 2, 24),
        send_near(rim_pay.at[1], rim_in.at[0], 3, 25),
    ]

    row_copies = [
        send_near(weighted_1.at[1], weighted_1.at[17], 0, 16),
        send_near(weighted_1.at[16], weighted_1.at[0], 1, 17),
    ]
    def ocean(first, last, tables=18):
        def block(j, carry):
            here = pl.ds(pl.multiple_of(j * 128, 128), 128)
            own = [tracer_ref[8 * g : 8 * g + 8, here] for g in range(4)]
            lateral = [jnp.zeros(TILE, F32) for g in range(4)]
            for e in range(6):
                idx = jnp.broadcast_to(near_ref[e : e + 1, here], TILE)
                coef = jnp.broadcast_to(coef_ref[e : e + 1, here], TILE)
                hi, lo = lax.shift_right_logical(idx, 7), lax.bitwise_and(idx, 127)
                found = [jnp.zeros(TILE, F32) for g in range(4)]
                for h in range(tables):
                    mine = hi == h
                    for g in range(4):
                        if h < 16:
                            tile = tracer_ref[8 * g : 8 * g + 8, 128 * h : 128 * h + 128]
                        else:
                            tile = rim_in[h - 16, 8 * g : 8 * g + 8, :]
                        found[g] = jnp.where(mine, jnp.take_along_axis(tile, lo, axis=1), found[g])
                for g in range(4):
                    lateral[g] = lateral[g] + coef * (found[g] - own[g])
            rate = jnp.broadcast_to(vert_ref[pl.ds(j, 1), :], TILE)
            for t in range(2):
                top, low = own[2 * t], own[2 * t + 1]
                down = [pltpu.roll(v, 1, 0) for v in (top, low)]
                up = [pltpu.roll(v, 7, 0) for v in (top, low)]
                above = [jnp.where(sub == 0, top, down[0]), jnp.where(sub == 0, down[0], down[1])]
                below = [jnp.where(sub == 7, up[1], up[0]), jnp.where(sub == 7, low, up[1])]
                for i, v in enumerate((top, low)):
                    g = 2 * t + i
                    vertical = rate * ((above[i] - v) + (below[i] - v))
                    ocean_out[8 * g : 8 * g + 8, here] = v + lateral[g] + vertical
            return carry

        lax.fori_loop(first, last, block, 0)

    def ocean_rim(first, last):
        def block(j, carry):
            here = pl.ds(pl.multiple_of(j * 128, 128), 128)
            lateral = [ocean_out[8 * g : 8 * g + 8, here] for g in range(4)]
            for e in range(6):
                idx = jnp.broadcast_to(near_ref[e : e + 1, here], TILE)
                coef = jnp.broadcast_to(coef_ref[e : e + 1, here], TILE)
                hi, lo = lax.shift_right_logical(idx, 7), lax.bitwise_and(idx, 127)
                for g in range(4):
                    found = jnp.zeros(TILE, F32)
                    for side in range(2):
                        tile = rim_in[side, 8 * g : 8 * g + 8, :]
                        found = jnp.where(
                            hi == 16 + side, jnp.take_along_axis(tile, lo, axis=1), found
                        )
                    lateral[g] = lateral[g] + coef * found
            for g in range(4):
                ocean_out[8 * g : 8 * g + 8, here] = lateral[g]
            return carry

        lax.fori_loop(first, last, block, 0)

    def sum_rows(weighted, column_pay):
        def group(g, carry):
            planes = pl.ds(pl.multiple_of(g * 8, 8), 8)
            packed = [jnp.zeros(TILE, F32), jnp.zeros(TILE, F32)]
            for x in range(16):
                total = weighted[x + 1, planes, :]
                if x % 4 == 0:
                    total = total + weighted[x, planes, :]
                if x % 4 == 3:
                    total = total + weighted[x + 2, planes, :]
                row_sum[x, planes, :] = total
                packed[0] = jnp.where(lane == x, pltpu.roll(total, x, 1), packed[0])
                packed[1] = jnp.where(lane == x, pltpu.roll(total, x + 1, 1), packed[1])
            for side in range(2):
                column_pay[side, planes, :] = packed[side]
            return carry

        lax.fori_loop(0, 6, group, 0)

    def sum_columns(column_in, store):
        def group(g, carry):
            planes = pl.ds(pl.multiple_of(g * 8, 8), 8)
            left, right = column_in[0, planes, :], column_in[1, planes, :]
            for x in range(16):
                v = row_sum[x, planes, :]
                before = jnp.where(
                    lane == 0, pltpu.roll(left, (128 - x) % 128, 1), pltpu.roll(v, 1, 1)
                )
                after = jnp.where(
                    lane == 127, pltpu.roll(right, 127 - x, 1), pltpu.roll(v, 127, 1)
                )
                total = v + jnp.where(first_y, before, 0.0) + jnp.where(last_y, after, 0.0)
                store(g, x, total * jnp.broadcast_to(inverse_ref[x : x + 1, :], TILE))
            return carry

        lax.fori_loop(0, 6, group, 0)

    build_hot(cols_ref, hot_cols)
    ocean(0, EARLY, 16)
    for copy in row_copies:
        copy.wait_recv()
    sum_rows(weighted_1, column_pay_1)
    column_copies = [
        send_near(column_pay_1.at[0], column_in_1.at[1], 2, 18),
        send_near(column_pay_1.at[1], column_in_1.at[0], 3, 19),
    ]

    for copy in margin_copies:
        copy.wait_recv()

    def widen(own, inbox):
        centre = [own[0:8], own[8:16], inbox(1)[0:8], inbox(0)[0:8]]
        right = [inbox(3)[0:8], inbox(3)[8:16], inbox(7)[0:8], inbox(5)[0:8]]
        left = [inbox(2)[0:8], inbox(2)[8:16], inbox(6)[0:8], inbox(4)[0:8]]
        return centre + [jnp.where(lane < 64, r, l) for r, l in zip(right, left)]

    def copy_sum(tiles):
        summed = []
        for side in range(2):
            part = tiles[4 * side : 4 * side + 4]
            prev = [pltpu.roll(v, 1, 0) for v in part]
            succ = [pltpu.roll(v, 7, 0) for v in part]
            for i in range(4):
                before = jnp.where(sub == 0, prev[i - 1], prev[i])
                after = jnp.where(sub == 7, succ[(i + 1) % 4], succ[i])
                summed.append(
                    part[i] + jnp.where(first_x, before, 0.0) + jnp.where(last_x, after, 0.0)
                )
        prev = [pltpu.roll(v, 1, 1) for v in summed]
        succ = [pltpu.roll(v, 127, 1) for v in summed]
        result = []
        for i in range(8):
            other = (i + 4) % 8
            before = jnp.where(lane == 0, prev[other], prev[i])
            after = jnp.where(lane == 127, succ[other], succ[i])
            result.append(
                summed[i] + jnp.where(first_y, before, 0.0) + jnp.where(last_y, after, 0.0)
            )
        return result

    taps_x = [(s, tap_table(x_pos, s)) for s in shifts]
    centre_x = tap_table(x_pos, 0)

    def without_surface(v, wind_x, wind_y):
        slope_x = centre_x * v
        for s, tap in taps_x:
            slope_x = slope_x + tap * pltpu.roll(v, (-s) % 8, 0)
        return v - F32(TIME_STEP) * (wind_x * slope_x + wind_y * slope_y(v)) - F32(RELAX) * v

    wide = [
        widen(margin_pay[q], lambda d, q=q: margin_in[d, q]) for q in range(4)
    ]
    wide_mass = [gll_weight * v for v in wide[3]]
    wide_inverse = [1.0 / v for v in copy_sum(wide_mass)]
    for i in range(8):
        base_ref[i] = without_surface(wide[0][i], wide[1][i], wide[2][i])
        wide_ref[0, i] = wide[1][i]
        wide_ref[1, i] = wide[2][i]
        wide_ref[2, i] = wide_mass[i]
        wide_ref[3, i] = wide_inverse[i]
    for half in range(2):
        inverse_ref[8 * half : 8 * half + 8, :] = wide_inverse[half]

    await_all(heat_in, all_recv.at[0])
    build_left(
        rows_ref,
        lambda base: (heat_in[pl.ds(base, 8), 0, :], heat_in[pl.ds(base, 8), 1, :]),
        left_ref,
    )
    heat, frac = scatter_sums(left_ref, hot_rows, 2)
    surf_pay[...] = (heat + land_ref[...] * air_ref[0:16, :]) / (frac + land_ref[...])
    for d in range(8):
        low, high = MARGIN_ROWS[DIRECTIONS[d][0]]
        surf_copies.append(
            send_near(
                surf_pay.at[low:high, :],
                surf_in.at[REVERSE[d], 0 : high - low, :],
                d,
                8 + d,
            )
        )

    for copy in column_copies:
        copy.wait_recv()

    def keep(g, x, v):
        field_1[x, pl.ds(pl.multiple_of(g * 8, 8), 8), :] = v

    sum_columns(column_in_1, keep)
    advance(lambda g, x: field_1[x, pl.ds(pl.multiple_of(g * 8, 8), 8), :], weighted_2)
    row_copies = [
        send_near(weighted_2.at[1], weighted_2.at[17], 0, 20),
        send_near(weighted_2.at[16], weighted_2.at[0], 1, 21),
    ]

    ocean(EARLY, EARLY + 1, 16)

    for copy in surf_copies:
        copy.wait_recv()
    surf = widen(surf_pay[...], lambda d: surf_in[d])
    moved = [
        wide_ref[2, i] * (base_ref[i] + F32(RELAX) * surf[i]) for i in range(8)
    ]
    field = [v * wide_ref[3, i] for i, v in enumerate(copy_sum(moved))]
    moved = [
        wide_ref[2, i]
        * (without_surface(field[i], wide_ref[0, i], wide_ref[1, i]) + F32(RELAX) * surf[i])
        for i in range(8)
    ]
    final = [v * wide_ref[3, i] for i, v in enumerate(copy_sum(moved)[0:2])]
    flux = [
        jnp.broadcast_to((final[h // 8] - surf[h // 8])[h % 8 : h % 8 + 1], TILE)
        for h in range(16)
    ]
    for i in range(n_blk // 8):
        idx = rows_ref[8 * i : 8 * i + 8, :]
        flux_pay[8 * i : 8 * i + 8, 0, :] = lane_gather(
            flux, lax.shift_right_logical(idx, 7), lax.bitwise_and(idx, 127)
        )
    exchange(flux_pay, flux_in, 1)
    flux_in[blk] = flux_pay[blk]

    for copy in rim_copies:
        copy.wait_recv()
    ocean(EARLY + 1, EARLY + 2)
    for copy in row_copies:
        copy.wait_recv()
    sum_rows(weighted_2, column_pay_2)
    column_copies = [
        send_near(column_pay_2.at[0], column_in_2.at[1], 2, 22),
        send_near(column_pay_2.at[1], column_in_2.at[0], 3, 23),
    ]
    ocean_rim(0, EARLY + 1)
    ocean(EARLY + 2, 13)
    for copy in column_copies:
        copy.wait_recv()

    def put_out(g, x, v):
        air_out[pl.ds(g * 128 + x, 8, stride=16), :] = v

    sum_columns(column_in_2, put_out)
    for half in range(2):
        air_out[8 * half : 8 * half + 8, :] = final[half]
    ocean(13, 16)

    await_all(flux_in, all_recv.at[1])
    build_left(
        cols_ref,
        lambda base: (weight_ref[pl.ds(base, 8), :] * flux_in[pl.ds(base, 8), 0, :],),
        left_ref,
    )
    (inflow,) = scatter_sums(left_ref, hot_cols, 1)
    gain = F32(FLUX_GAIN) * inflow / area_ref[...]
    for h in range(16):
        here = slice(128 * h, 128 * h + 128)
        ocean_out[0:1, here] = ocean_out[0:1, here] + gain[h : h + 1]

    for copy in started:
        copy.wait_send()
    await_all(heat_pay, all_send.at[0])
    await_all(flux_pay, all_send.at[1])


def solution(mesh):
    n_face, n_blk = mesh.shape["face"], mesh.shape["blk"]

    def body(
        air_state,
        air_wind,
        jacobian,
        land_area,
        xgrid_rows,
        tracers,
        edge_coef,
        neighbours,
        vert_rate,
        ocean_area,
        send_list,
        xgrid_cols,
        xgrid_weights,
    ):
        air_shape, ocean_shape = air_state.shape, tracers.shape
        vmem = pltpu.VMEM
        air, ocean = pl.pallas_call(
            lambda *refs: interval_kernel(n_face, n_blk, *refs),
            out_shape=(vmem((768, 128), F32), vmem((32, 2048), F32)),
            in_specs=[pl.BlockSpec(memory_space=pl.ANY)] * 13,
            out_specs=(pl.BlockSpec(memory_space=vmem),) * 2,
            scratch_shapes=[
                vmem((768, 128), F32),
                vmem((512, 128), F32),
                vmem((16, 128), F32),
                vmem((16, 128), F32),
                vmem((n_blk, 128), jnp.int32),
                vmem((32, 2048), F32),
                vmem((6, 2048), F32),
                vmem((6, 2048), jnp.int32),
                vmem((16, 128), F32),
                vmem((16, 128), F32),
                vmem((2, 128), jnp.int32),
                vmem((n_blk, 128), jnp.int32),
                vmem((n_blk, 128), F32),
                pltpu.SemaphoreType.DMA((13,)),
                vmem((n_blk, 2, 128), F32),
                vmem((n_blk, 2, 128), F32),
                vmem((n_blk, 1, 128), F32),
                vmem((n_blk, 1, 128), F32),
                vmem((2, 32, 128), F32),
                vmem((2, 32, 128), F32),
                vmem((4, 16, 128), F32),
                vmem((8, 4, 16, 128), F32),
                vmem((16, 128), F32),
                vmem((8, 16, 128), F32),
                vmem((18, 48, 128), F32),
                vmem((18, 48, 128), F32),
                vmem((16, 48, 128), F32),
                vmem((2, 48, 128), F32),
                vmem((2, 48, 128), F32),
                vmem((2, 48, 128), F32),
                vmem((2, 48, 128), F32),
                vmem((16, 48, 128), F32),
                vmem((16, 128), F32),
                vmem((16, 128), F32),
                vmem((128, 128 * n_blk), BF16),
                vmem((128, 128 * n_blk), BF16),
                vmem((32 * PARTS, 128 * n_blk), BF16),
                vmem((8, 8, 128), F32),
                vmem((4, 8, 8, 128), F32),
                pltpu.SemaphoreType.DMA((2,)),
                pltpu.SemaphoreType.DMA((2,)),
                pltpu.SemaphoreType.DMA((26,)),
                pltpu.SemaphoreType.DMA((26,)),
            ],
            compiler_params=pltpu.CompilerParams(collective_id=0, has_side_effects=True),
            name="interval",
        )(
            air_state.reshape(768, 128),
            air_wind.reshape(512, 128),
            jacobian,
            land_area,
            xgrid_rows[0],
            tracers.reshape(32, 2048),
            edge_coef,
            neighbours,
            vert_rate.reshape(16, 128),
            ocean_area.reshape(16, 128),
            send_list.reshape(2, 128),
            xgrid_cols[0],
            xgrid_weights[0],
        )
        return air.reshape(air_shape), ocean.reshape(ocean_shape)

    both = ("face", "blk")
    in_specs = (
        P(None, None, "face", "blk"),
        P(None, None, "face", "blk"),
        P("face", "blk"),
        P("face", "blk"),
        P(both, None, None),
        P(None, None, both),
        P(None, both),
        P(None, both),
        P(both),
        P(both),
        P(both, None),
        P(both, None, None),
        P(both, None, None),
    )
    out_specs = (P(None, None, "face", "blk"), P(None, None, both))
    return jax.shard_map(body, mesh=mesh, in_specs=in_specs, out_specs=out_specs, check_vma=False)
```

```python
import jax
import jax.numpy as jnp
from jax import lax
from jax.experimental import pallas as pl
from jax.experimental.pallas import tpu as pltpu
from jax.sharding import PartitionSpec as P

GLL = 4
DERIV = (
    (-3.0, 4.045084971874737, -1.545084971874737, 0.5),
    (-0.8090169943749475, 0.0, 1.118033988749895, -0.30901699437494745),
    (0.30901699437494745, -1.118033988749895, 0.0, 0.8090169943749475),
    (-0.5, 1.545084971874737, -4.045084971874737, 3.0),
)
TIME_STEP = 0.05
RELAX = 0.3
FLUX_GAIN = 0.2
DIRECTIONS = ((-1, 0), (1, 0), (0, -1), (0, 1), (-1, -1), (-1, 1), (1, -1), (1, 1))
REVERSE = (1, 0, 3, 2, 7, 6, 5, 4)
MARGIN_ROWS = {-1: (0, 8), 1: (8, 16), 0: (0, 16)}
MESH = pl.DeviceIdType.MESH
F32 = jnp.float32
BF16 = jnp.bfloat16
TILE = (8, 128)
PARTS = 2
EARLY = 5


def lane_gather(rows, hi, lo):
    found = jnp.zeros(TILE, F32)
    for h, row in enumerate(rows):
        found = jnp.where(hi == h, jnp.take_along_axis(row, lo, axis=1), found)
    return found


def tap_table(position, shift):
    table = jnp.zeros(TILE, F32)
    for i in range(GLL):
        if 0 <= i + shift < GLL:
            table = jnp.where(position == i, F32(DERIV[i][i + shift]), table)
    return table


def build_hot(idx_ref, hot_ref):
    rows = lax.broadcasted_iota(jnp.int32, (128, 128), 0)

    def step(r8, carry):
        base = pl.multiple_of(r8 * 8, 8)
        for i in range(8):
            lo = lax.bitwise_and(idx_ref[pl.ds(base + i, 1), :], 127)
            hot = jnp.where(rows == jnp.broadcast_to(lo, (128, 128)), 1.0, 0.0).astype(BF16)
            hot_ref[:, pl.ds(pl.multiple_of((base + i) * 128, 128), 128)] = hot
        return carry

    lax.fori_loop(0, idx_ref.shape[0] // 8, step, 0)


def build_left(idx_ref, values_at, left_ref):
    rows = lax.broadcasted_iota(jnp.int32, (16, 128), 0)

    def step(r8, carry):
        base = pl.multiple_of(r8 * 8, 8)
        hi = lax.shift_right_logical(idx_ref[pl.ds(base, 8), :], 7)
        parts = []
        for rest in values_at(base):
            for _ in range(PARTS):
                part = rest.astype(BF16).astype(F32)
                parts.append(part)
                rest = rest - part
        for i in range(8):
            mine = jnp.broadcast_to(hi[i : i + 1], (16, 128)) == rows
            left = [
                jnp.where(mine, jnp.broadcast_to(p[i : i + 1], (16, 128)), 0.0).astype(BF16)
                for p in parts
            ]
            left_ref[0 : 16 * len(parts), pl.ds(pl.multiple_of((base + i) * 128, 128), 128)] = (
                jnp.concatenate(left, axis=0)
            )
        return carry

    lax.fori_loop(0, idx_ref.shape[0] // 8, step, 0)


def scatter_sums(left_ref, hot_ref, count):
    size = 16 * PARTS
    total = lax.dot_general(
        left_ref[0 : size * count, :],
        hot_ref[...],
        (((1,), (1,)), ((), ())),
        preferred_element_type=F32,
    )
    return [
        sum(total[size * q + 16 * p : size * q + 16 * p + 16] for p in range(PARTS))
        for q in range(count)
    ]


def interval_kernel(
    n_face,
    n_blk,
    air_hbm,
    wind_hbm,
    jac_hbm,
    land_hbm,
    rows_hbm,
    tracer_hbm,
    coef_hbm,
    near_hbm,
    vert_hbm,
    send_hbm,
    cols_hbm,
    weight_hbm,
    air_out,
    ocean_out,
    left_out,
    hot_cols,
    air_ref,
    wind_ref,
    jac_ref,
    land_ref,
    rows_ref,
    tracer_ref,
    coef_ref,
    near_ref,
    vert_ref,
    send_ref,
    cols_ref,
    weight_ref,
    load_sem,
    heat_pay,
    heat_in,
    flux_pay,
    flux_in,
    rim_pay,
    rim_in,
    margin_pay,
    margin_in,
    surf_pay,
    surf_in,
    weighted_1,
    weighted_2,
    row_sum,
    column_pay_1,
    column_in_1,
    column_pay_2,
    column_in_2,
    field_1,
    mass_ref,
    inverse_ref,
    hot_rows,
    left_ref,
    base_ref,
    wide_ref,
    all_send,
    all_recv,
    near_send,
    near_recv,
):
    face, blk = lax.axis_index("face"), lax.axis_index("blk")

    def step_to(d):
        df, db = DIRECTIONS[d]
        return (lax.rem(face + df + n_face, n_face), lax.rem(blk + db + n_blk, n_blk))

    names = (
        *("cols", "weight", "tracer", "send", "air", "wind", "jac"),
        *("rows", "land", "coef", "near", "vert"),
    )
    pairs = {
        "air": (air_hbm, air_ref),
        "wind": (wind_hbm, wind_ref),
        "jac": (jac_hbm, jac_ref),
        "land": (land_hbm, land_ref),
        "rows": (rows_hbm, rows_ref),
        "tracer": (tracer_hbm, tracer_ref),
        "coef": (coef_hbm, coef_ref),
        "near": (near_hbm, near_ref),
        "vert": (vert_hbm, vert_ref),
        "send": (send_hbm, send_ref),
        "cols": (cols_hbm, cols_ref),
        "weight": (weight_hbm, weight_ref),
    }
    loads = {
        name: pltpu.make_async_copy(*pairs[name], load_sem.at[i]) for i, name in enumerate(names)
    }
    for name in names:
        loads[name].start()

    def loaded(*wanted):
        for name in wanted:
            loads[name].wait()

    def every_peer(act):
        half = n_blk // 2
        act(lax.rem(blk + half, n_blk))

        def both(k, carry):
            act(lax.rem(blk + half + k, n_blk))
            act(lax.rem(blk + half - k, n_blk))
            return carry

        lax.fori_loop(1, half, both, 0)

    barrier = pltpu.get_barrier_semaphore()
    for d in (4, 5, 6, 7, 0, 1):
        pl.semaphore_signal(barrier, inc=1, device_id=step_to(d), device_id_type=MESH)
    every_peer(
        lambda peer: pl.semaphore_signal(
            barrier, inc=1, device_id=(face, peer), device_id_type=MESH
        )
    )

    sub = lax.broadcasted_iota(jnp.int32, TILE, 0)
    lane = lax.broadcasted_iota(jnp.int32, TILE, 1)
    x_pos, y_pos = lax.bitwise_and(sub, 3), lax.bitwise_and(lane, 3)
    first_x, last_x = x_pos == 0, x_pos == 3
    first_y, last_y = y_pos == 0, y_pos == 3
    sixth, five_sixths = F32(1.0 / 6.0), F32(5.0 / 6.0)
    gll_weight = jnp.where(first_x | last_x, sixth, five_sixths) * jnp.where(
        first_y | last_y, sixth, five_sixths
    )
    shifts = (-3, -2, -1, 1, 2, 3)

    loaded("cols", "weight", "tracer")
    surface = [
        jnp.broadcast_to(tracer_ref[0:1, 128 * h : 128 * h + 128], TILE) for h in range(16)
    ]
    for i in range(n_blk // 8):
        idx = cols_ref[8 * i : 8 * i + 8, :]
        weight = weight_ref[8 * i : 8 * i + 8, :]
        at = lane_gather(surface, lax.shift_right_logical(idx, 7), lax.bitwise_and(idx, 127))
        heat_pay[8 * i : 8 * i + 8, 0, :] = weight * at
        heat_pay[8 * i : 8 * i + 8, 1, :] = weight

    loaded("air", "wind", "jac")
    margin_pay[0] = air_ref[0:16, :]
    margin_pay[1] = wind_ref[0:16, :]
    margin_pay[2] = wind_ref[256:272, :]
    margin_pay[3] = jac_ref[...]
    for half in range(2):
        mass_ref[8 * half : 8 * half + 8, :] = gll_weight * jac_ref[8 * half : 8 * half + 8, :]

    loaded("send")
    for side in range(2):
        idx = jnp.broadcast_to(send_ref[side : side + 1, :], TILE)
        hi, lo = lax.shift_right_logical(idx, 7), lax.bitwise_and(idx, 127)
        for g in range(4):
            tiles = [tracer_ref[8 * g : 8 * g + 8, 128 * h : 128 * h + 128] for h in range(16)]
            rim_pay[side, 8 * g : 8 * g + 8, :] = lane_gather(tiles, hi, lo)

    taps_y = [(s, tap_table(y_pos, s)) for s in shifts]
    centre_y = tap_table(y_pos, 0)

    def slope_y(v):
        total = centre_y * v
        for s, tap in taps_y:
            total = total + tap * pltpu.roll(v, (-s) % 128, 1)
        return total

    def advance(field_at, target):
        def group(g, carry):
            half = lax.rem(g, 2) * 128
            planes = pl.ds(pl.multiple_of(g * 8, 8), 8)
            for e in range(4):
                fields = [field_at(g, 4 * e + k) for k in range(4)]
                for i in range(4):
                    x = 4 * e + i
                    slope_x = None
                    for k in range(4):
                        if DERIV[i][k]:
                            term = F32(DERIV[i][k]) * fields[k]
                            slope_x = term if slope_x is None else slope_x + term
                    wind_x = wind_ref[pl.ds(half + x, 8, stride=16), :]
                    wind_y = wind_ref[pl.ds(half + 256 + x, 8, stride=16), :]
                    tendency = wind_x * slope_x + wind_y * slope_y(fields[i])
                    moved = fields[i] - F32(TIME_STEP) * tendency
                    mass = jnp.broadcast_to(mass_ref[x : x + 1, :], TILE)
                    target[x + 1, planes, :] = mass * moved
            return carry

        lax.fori_loop(0, 6, group, 0)

    advance(lambda g, x: air_ref[pl.ds(g * 128 + x, 8, stride=16), :], weighted_1)
    loaded("rows", "land", "coef", "near", "vert")
    build_hot(rows_ref, hot_rows)

    pl.semaphore_wait(barrier, n_blk - 1 + 6)

    def exchange(pay, inbox, slot):
        every_peer(
            lambda peer: pltpu.make_async_remote_copy(
                src_ref=pay.at[peer],
                dst_ref=inbox.at[blk],
                send_sem=all_send.at[slot],
                recv_sem=all_recv.at[slot],
                device_id=(face, peer),
                device_id_type=MESH,
            ).start()
        )

    def await_all(ref, sem):
        rest = ref.at[pl.ds(0, n_blk - 1)]
        pltpu.make_async_copy(rest, rest, sem).wait()

    started = []

    def send_near(src, dst, d, slot):
        copy = pltpu.make_async_remote_copy(
            src_ref=src,
            dst_ref=dst,
            send_sem=near_send.at[slot],
            recv_sem=near_recv.at[slot],
            device_id=step_to(d),
            device_id_type=MESH,
        )
        copy.start()
        started.append(copy)
        return copy

    exchange(heat_pay, heat_in, 0)
    heat_in[blk] = heat_pay[blk]

    margin_copies, surf_copies = [], []
    for d in range(8):
        low, high = MARGIN_ROWS[DIRECTIONS[d][0]]
        margin_copies.append(
            send_near(
                margin_pay.at[:, low:high, :],
                margin_in.at[REVERSE[d], :, 0 : high - low, :],
                d,
                d,
            )
        )

    rim_copies = [
        send_near(rim_pay.at[0], rim_in.at[1], 2, 24),
        send_near(rim_pay.at[1], rim_in.at[0], 3, 25),
    ]

    row_copies = [
        send_near(weighted_1.at[1], weighted_1.at[17], 0, 16),
        send_near(weighted_1.at[16], weighted_1.at[0], 1, 17),
    ]
    def ocean(first, last, tables=18):
        def block(j, carry):
            here = pl.ds(pl.multiple_of(j * 128, 128), 128)
            own = [tracer_ref[8 * g : 8 * g + 8, here] for g in range(4)]
            lateral = [jnp.zeros(TILE, F32) for g in range(4)]
            for e in range(6):
                idx = jnp.broadcast_to(near_ref[e : e + 1, here], TILE)
                coef = jnp.broadcast_to(coef_ref[e : e + 1, here], TILE)
                hi, lo = lax.shift_right_logical(idx, 7), lax.bitwise_and(idx, 127)
                found = [jnp.zeros(TILE, F32) for g in range(4)]
                for h in range(tables):
                    mine = hi == h
                    for g in range(4):
                        if h < 16:
                            tile = tracer_ref[8 * g : 8 * g + 8, 128 * h : 128 * h + 128]
                        else:
                            tile = rim_in[h - 16, 8 * g : 8 * g + 8, :]
                        found[g] = jnp.where(mine, jnp.take_along_axis(tile, lo, axis=1), found[g])
                for g in range(4):
                    lateral[g] = lateral[g] + coef * (found[g] - own[g])
            rate = jnp.broadcast_to(vert_ref[pl.ds(j, 1), :], TILE)
            for t in range(2):
                top, low = own[2 * t], own[2 * t + 1]
                down = [pltpu.roll(v, 1, 0) for v in (top, low)]
                up = [pltpu.roll(v, 7, 0) for v in (top, low)]
                above = [jnp.where(sub == 0, top, down[0]), jnp.where(sub == 0, down[0], down[1])]
                below = [jnp.where(sub == 7, up[1], up[0]), jnp.where(sub == 7, low, up[1])]
                for i, v in enumerate((top, low)):
                    g = 2 * t + i
                    vertical = rate * ((above[i] - v) + (below[i] - v))
                    ocean_out[8 * g : 8 * g + 8, here] = v + lateral[g] + vertical
            return carry

        lax.fori_loop(first, last, block, 0)

    def ocean_rim(first, last):
        def block(j, carry):
            here = pl.ds(pl.multiple_of(j * 128, 128), 128)
            lateral = [ocean_out[8 * g : 8 * g + 8, here] for g in range(4)]
            for e in range(6):
                idx = jnp.broadcast_to(near_ref[e : e + 1, here], TILE)
                coef = jnp.broadcast_to(coef_ref[e : e + 1, here], TILE)
                hi, lo = lax.shift_right_logical(idx, 7), lax.bitwise_and(idx, 127)
                for g in range(4):
                    found = jnp.zeros(TILE, F32)
                    for side in range(2):
                        tile = rim_in[side, 8 * g : 8 * g + 8, :]
                        found = jnp.where(
                            hi == 16 + side, jnp.take_along_axis(tile, lo, axis=1), found
                        )
                    lateral[g] = lateral[g] + coef * found
            for g in range(4):
                ocean_out[8 * g : 8 * g + 8, here] = lateral[g]
            return carry

        lax.fori_loop(first, last, block, 0)

    def sum_rows(weighted, column_pay):
        def group(g, carry):
            planes = pl.ds(pl.multiple_of(g * 8, 8), 8)
            packed = [jnp.zeros(TILE, F32), jnp.zeros(TILE, F32)]
            for x in range(16):
                total = weighted[x + 1, planes, :]
                if x % 4 == 0:
                    total = total + weighted[x, planes, :]
                if x % 4 == 3:
                    total = total + weighted[x + 2, planes, :]
                row_sum[x, planes, :] = total
                packed[0] = jnp.where(lane == x, pltpu.roll(total, x, 1), packed[0])
                packed[1] = jnp.where(lane == x, pltpu.roll(total, x + 1, 1), packed[1])
            for side in range(2):
                column_pay[side, planes, :] = packed[side]
            return carry

        lax.fori_loop(0, 6, group, 0)

    def sum_columns(column_in, store):
        def group(g, carry):
            planes = pl.ds(pl.multiple_of(g * 8, 8), 8)
            left, right = column_in[0, planes, :], column_in[1, planes, :]
            for x in range(16):
                v = row_sum[x, planes, :]
                before = jnp.where(
                    lane == 0, pltpu.roll(left, (128 - x) % 128, 1), pltpu.roll(v, 1, 1)
                )
                after = jnp.where(
                    lane == 127, pltpu.roll(right, 127 - x, 1), pltpu.roll(v, 127, 1)
                )
                total = v + jnp.where(first_y, before, 0.0) + jnp.where(last_y, after, 0.0)
                store(g, x, total * jnp.broadcast_to(inverse_ref[x : x + 1, :], TILE))
            return carry

        lax.fori_loop(0, 6, group, 0)

    build_hot(cols_ref, hot_cols)
    ocean(0, EARLY, 16)
    for copy in row_copies:
        copy.wait_recv()
    sum_rows(weighted_1, column_pay_1)
    column_copies = [
        send_near(column_pay_1.at[0], column_in_1.at[1], 2, 18),
        send_near(column_pay_1.at[1], column_in_1.at[0], 3, 19),
    ]

    for copy in margin_copies:
        copy.wait_recv()

    def widen(own, inbox):
        centre = [own[0:8], own[8:16], inbox(1)[0:8], inbox(0)[0:8]]
        right = [inbox(3)[0:8], inbox(3)[8:16], inbox(7)[0:8], inbox(5)[0:8]]
        left = [inbox(2)[0:8], inbox(2)[8:16], inbox(6)[0:8], inbox(4)[0:8]]
        return centre + [jnp.where(lane < 64, r, l) for r, l in zip(right, left)]

    def copy_sum(tiles):
        summed = []
        for side in range(2):
            part = tiles[4 * side : 4 * side + 4]
            prev = [pltpu.roll(v, 1, 0) for v in part]
            succ = [pltpu.roll(v, 7, 0) for v in part]
            for i in range(4):
                before = jnp.where(sub == 0, prev[i - 1], prev[i])
                after = jnp.where(sub == 7, succ[(i + 1) % 4], succ[i])
                summed.append(
                    part[i] + jnp.where(first_x, before, 0.0) + jnp.where(last_x, after, 0.0)
                )
        prev = [pltpu.roll(v, 1, 1) for v in summed]
        succ = [pltpu.roll(v, 127, 1) for v in summed]
        result = []
        for i in range(8):
            other = (i + 4) % 8
            before = jnp.where(lane == 0, prev[other], prev[i])
            after = jnp.where(lane == 127, succ[other], succ[i])
            result.append(
                summed[i] + jnp.where(first_y, before, 0.0) + jnp.where(last_y, after, 0.0)
            )
        return result

    taps_x = [(s, tap_table(x_pos, s)) for s in shifts]
    centre_x = tap_table(x_pos, 0)

    def without_surface(v, wind_x, wind_y):
        slope_x = centre_x * v
        for s, tap in taps_x:
            slope_x = slope_x + tap * pltpu.roll(v, (-s) % 8, 0)
        return v - F32(TIME_STEP) * (wind_x * slope_x + wind_y * slope_y(v)) - F32(RELAX) * v

    wide = [
        widen(margin_pay[q], lambda d, q=q: margin_in[d, q]) for q in range(4)
    ]
    wide_mass = [gll_weight * v for v in wide[3]]
    wide_inverse = [1.0 / v for v in copy_sum(wide_mass)]
    for i in range(8):
        base_ref[i] = without_surface(wide[0][i], wide[1][i], wide[2][i])
        wide_ref[0, i] = wide[1][i]
        wide_ref[1, i] = wide[2][i]
        wide_ref[2, i] = wide_mass[i]
        wide_ref[3, i] = wide_inverse[i]
    for half in range(2):
        inverse_ref[8 * half : 8 * half + 8, :] = wide_inverse[half]

    await_all(heat_in, all_recv.at[0])
    build_left(
        rows_ref,
        lambda base: (heat_in[pl.ds(base, 8), 0, :], heat_in[pl.ds(base, 8), 1, :]),
        left_ref,
    )
    heat, frac = scatter_sums(left_ref, hot_rows, 2)
    surf_pay[...] = (heat + land_ref[...] * air_ref[0:16, :]) / (frac + land_ref[...])
    for d in range(8):
        low, high = MARGIN_ROWS[DIRECTIONS[d][0]]
        surf_copies.append(
            send_near(
                surf_pay.at[low:high, :],
                surf_in.at[REVERSE[d], 0 : high - low, :],
                d,
                8 + d,
            )
        )

    for copy in column_copies:
        copy.wait_recv()

    def keep(g, x, v):
        field_1[x, pl.ds(pl.multiple_of(g * 8, 8), 8), :] = v

    sum_columns(column_in_1, keep)
    advance(lambda g, x: field_1[x, pl.ds(pl.multiple_of(g * 8, 8), 8), :], weighted_2)
    row_copies = [
        send_near(weighted_2.at[1], weighted_2.at[17], 0, 20),
        send_near(weighted_2.at[16], weighted_2.at[0], 1, 21),
    ]

    ocean(EARLY, EARLY + 1, 16)

    for copy in surf_copies:
        copy.wait_recv()
    surf = widen(surf_pay[...], lambda d: surf_in[d])
    moved = [
        wide_ref[2, i] * (base_ref[i] + F32(RELAX) * surf[i]) for i in range(8)
    ]
    field = [v * wide_ref[3, i] for i, v in enumerate(copy_sum(moved))]
    moved = [
        wide_ref[2, i]
        * (without_surface(field[i], wide_ref[0, i], wide_ref[1, i]) + F32(RELAX) * surf[i])
        for i in range(8)
    ]
    final = [v * wide_ref[3, i] for i, v in enumerate(copy_sum(moved)[0:2])]
    flux = [
        jnp.broadcast_to((final[h // 8] - surf[h // 8])[h % 8 : h % 8 + 1], TILE)
        for h in range(16)
    ]
    for i in range(n_blk // 8):
        idx = rows_ref[8 * i : 8 * i + 8, :]
        flux_pay[8 * i : 8 * i + 8, 0, :] = lane_gather(
            flux, lax.shift_right_logical(idx, 7), lax.bitwise_and(idx, 127)
        )
    exchange(flux_pay, flux_in, 1)
    flux_in[blk] = flux_pay[blk]

    for copy in rim_copies:
        copy.wait_recv()
    ocean(EARLY + 1, EARLY + 2)
    for copy in row_copies:
        copy.wait_recv()
    sum_rows(weighted_2, column_pay_2)
    column_copies = [
        send_near(column_pay_2.at[0], column_in_2.at[1], 2, 22),
        send_near(column_pay_2.at[1], column_in_2.at[0], 3, 23),
    ]
    ocean_rim(0, EARLY + 1)
    ocean(EARLY + 2, 13)
    for copy in column_copies:
        copy.wait_recv()

    def put_out(g, x, v):
        air_out[pl.ds(g * 128 + x, 8, stride=16), :] = v

    sum_columns(column_in_2, put_out)
    for half in range(2):
        air_out[8 * half : 8 * half + 8, :] = final[half]
    ocean(13, 16)

    await_all(flux_in, all_recv.at[1])
    build_left(
        cols_ref,
        lambda base: (weight_ref[pl.ds(base, 8), :] * flux_in[pl.ds(base, 8), 0, :],),
        left_out,
    )
    for copy in started:
        copy.wait_send()
    await_all(heat_pay, all_send.at[0])
    await_all(flux_pay, all_send.at[1])


def finish_kernel(air_ref, ocean_ref, left_ref, hot_ref, area_ref, air_out, ocean_out, top, sem):
    air_copy = pltpu.make_async_copy(air_ref, air_out, sem.at[0])
    ocean_copy = pltpu.make_async_copy(
        ocean_ref.at[pl.ds(8, 24), :], ocean_out.at[pl.ds(8, 24), :], sem.at[1]
    )
    air_copy.start()
    ocean_copy.start()
    (inflow,) = scatter_sums(left_ref, hot_ref, 1)
    gain = F32(FLUX_GAIN) * inflow / area_ref[...]
    first = lax.broadcasted_iota(jnp.int32, TILE, 0) == 0
    for h in range(16):
        here = slice(128 * h, 128 * h + 128)
        add = jnp.where(first, jnp.broadcast_to(gain[h : h + 1], TILE), 0.0)
        top[:, here] = ocean_ref[0:8, here] + add
    top_copy = pltpu.make_async_copy(top, ocean_out.at[pl.ds(0, 8), :], sem.at[2])
    top_copy.start()
    for copy in (air_copy, ocean_copy, top_copy):
        copy.wait()


def solution(mesh):
    n_face, n_blk = mesh.shape["face"], mesh.shape["blk"]

    def body(
        air_state,
        air_wind,
        jacobian,
        land_area,
        xgrid_rows,
        tracers,
        edge_coef,
        neighbours,
        vert_rate,
        ocean_area,
        send_list,
        xgrid_cols,
        xgrid_weights,
    ):
        air_shape, ocean_shape = air_state.shape, tracers.shape
        vmem = pltpu.VMEM
        air, ocean, left, hot = pl.pallas_call(
            lambda *refs: interval_kernel(n_face, n_blk, *refs),
            out_shape=(
                vmem((768, 128), F32),
                vmem((32, 2048), F32),
                vmem((16 * PARTS, 128 * n_blk), BF16),
                vmem((128, 128 * n_blk), BF16),
            ),
            in_specs=[pl.BlockSpec(memory_space=pl.ANY)] * 12,
            out_specs=(pl.BlockSpec(memory_space=vmem),) * 4,
            scratch_shapes=[
                vmem((768, 128), F32),
                vmem((512, 128), F32),
                vmem((16, 128), F32),
                vmem((16, 128), F32),
                vmem((n_blk, 128), jnp.int32),
                vmem((32, 2048), F32),
                vmem((6, 2048), F32),
                vmem((6, 2048), jnp.int32),
                vmem((16, 128), F32),
                vmem((2, 128), jnp.int32),
                vmem((n_blk, 128), jnp.int32),
                vmem((n_blk, 128), F32),
                pltpu.SemaphoreType.DMA((12,)),
                vmem((n_blk, 2, 128), F32),
                vmem((n_blk, 2, 128), F32),
                vmem((n_blk, 1, 128), F32),
                vmem((n_blk, 1, 128), F32),
                vmem((2, 32, 128), F32),
                vmem((2, 32, 128), F32),
                vmem((4, 16, 128), F32),
                vmem((8, 4, 16, 128), F32),
                vmem((16, 128), F32),
                vmem((8, 16, 128), F32),
                vmem((18, 48, 128), F32),
                vmem((18, 48, 128), F32),
                vmem((16, 48, 128), F32),
                vmem((2, 48, 128), F32),
                vmem((2, 48, 128), F32),
                vmem((2, 48, 128), F32),
                vmem((2, 48, 128), F32),
                vmem((16, 48, 128), F32),
                vmem((16, 128), F32),
                vmem((16, 128), F32),
                vmem((128, 128 * n_blk), BF16),
                vmem((32 * PARTS, 128 * n_blk), BF16),
                vmem((8, 8, 128), F32),
                vmem((4, 8, 8, 128), F32),
                pltpu.SemaphoreType.DMA((2,)),
                pltpu.SemaphoreType.DMA((2,)),
                pltpu.SemaphoreType.DMA((26,)),
                pltpu.SemaphoreType.DMA((26,)),
            ],
            compiler_params=pltpu.CompilerParams(collective_id=0, has_side_effects=True),
            name="interval",
        )(
            air_state.reshape(768, 128),
            air_wind.reshape(512, 128),
            jacobian,
            land_area,
            xgrid_rows[0],
            tracers.reshape(32, 2048),
            edge_coef,
            neighbours,
            vert_rate.reshape(16, 128),
            send_list.reshape(2, 128),
            xgrid_cols[0],
            xgrid_weights[0],
        )
        air, ocean = pl.pallas_call(
            finish_kernel,
            out_shape=(
                jax.ShapeDtypeStruct((768, 128), F32),
                jax.ShapeDtypeStruct((32, 2048), F32),
            ),
            in_specs=[pl.BlockSpec(memory_space=vmem)] * 5,
            out_specs=(pl.BlockSpec(memory_space=pl.ANY),) * 2,
            scratch_shapes=[vmem((8, 2048), F32), pltpu.SemaphoreType.DMA((3,))],
            name="finish",
        )(*(pltpu.with_memory_space_constraint(v, vmem) for v in (air, ocean, left, hot)), ocean_area.reshape(16, 128))
        return air.reshape(air_shape), ocean.reshape(ocean_shape)

    both = ("face", "blk")
    in_specs = (
        P(None, None, "face", "blk"),
        P(None, None, "face", "blk"),
        P("face", "blk"),
        P("face", "blk"),
        P(both, None, None),
        P(None, None, both),
        P(None, both),
        P(None, both),
        P(both),
        P(both),
        P(both, None),
        P(both, None, None),
        P(both, None, None),
    )
    out_specs = (P(None, None, "face", "blk"), P(None, None, both))
    return jax.shard_map(body, mesh=mesh, in_specs=in_specs, out_specs=out_specs, check_vma=False)
```

```python
import jax
import jax.numpy as jnp
from jax import lax
from jax.experimental import pallas as pl
from jax.experimental.pallas import tpu as pltpu
from jax.sharding import PartitionSpec as P

GLL = 4
DERIV = (
    (-3.0, 4.045084971874737, -1.545084971874737, 0.5),
    (-0.8090169943749475, 0.0, 1.118033988749895, -0.30901699437494745),
    (0.30901699437494745, -1.118033988749895, 0.0, 0.8090169943749475),
    (-0.5, 1.545084971874737, -4.045084971874737, 3.0),
)
TIME_STEP = 0.05
RELAX = 0.3
FLUX_GAIN = 0.2
DIRECTIONS = ((-1, 0), (1, 0), (0, -1), (0, 1), (-1, -1), (-1, 1), (1, -1), (1, 1))
REVERSE = (1, 0, 3, 2, 7, 6, 5, 4)
MARGIN_ROWS = {-1: (0, 8), 1: (8, 16), 0: (0, 16)}
MESH = pl.DeviceIdType.MESH
F32 = jnp.float32
BF16 = jnp.bfloat16
TILE = (8, 128)
PARTS = 2
EARLY = 5


def lane_gather(rows, hi, lo):
    found = jnp.zeros(TILE, F32)
    for h, row in enumerate(rows):
        found = jnp.where(hi == h, jnp.take_along_axis(row, lo, axis=1), found)
    return found


def tap_table(position, shift):
    table = jnp.zeros(TILE, F32)
    for i in range(GLL):
        if 0 <= i + shift < GLL:
            table = jnp.where(position == i, F32(DERIV[i][i + shift]), table)
    return table


def build_hot(idx_ref, hot_ref):
    rows = lax.broadcasted_iota(jnp.int32, (128, 128), 0)

    def step(r8, carry):
        base = pl.multiple_of(r8 * 8, 8)
        for i in range(8):
            lo = lax.bitwise_and(idx_ref[pl.ds(base + i, 1), :], 127)
            hot = jnp.where(rows == jnp.broadcast_to(lo, (128, 128)), 1.0, 0.0).astype(BF16)
            hot_ref[:, pl.ds(pl.multiple_of((base + i) * 128, 128), 128)] = hot
        return carry

    lax.fori_loop(0, idx_ref.shape[0] // 8, step, 0)


def build_left(idx_ref, values_at, left_ref):
    rows = lax.broadcasted_iota(jnp.int32, (16, 128), 0)

    def step(r8, carry):
        base = pl.multiple_of(r8 * 8, 8)
        hi = lax.shift_right_logical(idx_ref[pl.ds(base, 8), :], 7)
        parts = []
        for rest in values_at(base):
            for _ in range(PARTS):
                part = rest.astype(BF16).astype(F32)
                parts.append(part)
                rest = rest - part
        for i in range(8):
            mine = jnp.broadcast_to(hi[i : i + 1], (16, 128)) == rows
            left = [
                jnp.where(mine, jnp.broadcast_to(p[i : i + 1], (16, 128)), 0.0).astype(BF16)
                for p in parts
            ]
            left_ref[0 : 16 * len(parts), pl.ds(pl.multiple_of((base + i) * 128, 128), 128)] = (
                jnp.concatenate(left, axis=0)
            )
        return carry

    lax.fori_loop(0, idx_ref.shape[0] // 8, step, 0)


def scatter_sums(left_ref, hot_ref, count):
    size = 16 * PARTS
    total = lax.dot_general(
        left_ref[0 : size * count, :],
        hot_ref[...],
        (((1,), (1,)), ((), ())),
        preferred_element_type=F32,
    )
    return [
        sum(total[size * q + 16 * p : size * q + 16 * p + 16] for p in range(PARTS))
        for q in range(count)
    ]


def interval_kernel(
    n_face,
    n_blk,
    air_hbm,
    wind_hbm,
    jac_hbm,
    land_hbm,
    rows_hbm,
    tracer_hbm,
    coef_hbm,
    near_hbm,
    vert_hbm,
    area_hbm,
    send_hbm,
    cols_hbm,
    weight_hbm,
    air_out,
    ocean_out,
    left_out,
    hot_cols,
    area_out,
    air_ref,
    wind_ref,
    jac_ref,
    land_ref,
    rows_ref,
    tracer_ref,
    coef_ref,
    near_ref,
    vert_ref,
    send_ref,
    cols_ref,
    weight_ref,
    load_sem,
    heat_pay,
    heat_in,
    flux_pay,
    flux_in,
    rim_pay,
    rim_in,
    margin_pay,
    margin_in,
    surf_pay,
    surf_in,
    weighted_1,
    weighted_2,
    row_sum,
    column_pay_1,
    column_in_1,
    column_pay_2,
    column_in_2,
    field_1,
    mass_ref,
    inverse_ref,
    hot_rows,
    left_ref,
    base_ref,
    wide_ref,
    all_send,
    all_recv,
    near_send,
    near_recv,
):
    face, blk = lax.axis_index("face"), lax.axis_index("blk")

    def step_to(d):
        df, db = DIRECTIONS[d]
        return (lax.rem(face + df + n_face, n_face), lax.rem(blk + db + n_blk, n_blk))

    names = (
        *("cols", "weight", "tracer", "send", "air", "wind", "jac"),
        *("rows", "land", "coef", "near", "vert", "area"),
    )
    pairs = {
        "air": (air_hbm, air_ref),
        "wind": (wind_hbm, wind_ref),
        "jac": (jac_hbm, jac_ref),
        "land": (land_hbm, land_ref),
        "rows": (rows_hbm, rows_ref),
        "tracer": (tracer_hbm, tracer_ref),
        "coef": (coef_hbm, coef_ref),
        "near": (near_hbm, near_ref),
        "vert": (vert_hbm, vert_ref),
        "area": (area_hbm, area_out),
        "send": (send_hbm, send_ref),
        "cols": (cols_hbm, cols_ref),
        "weight": (weight_hbm, weight_ref),
    }
    loads = {
        name: pltpu.make_async_copy(*pairs[name], load_sem.at[i]) for i, name in enumerate(names)
    }
    for name in names:
        loads[name].start()

    def loaded(*wanted):
        for name in wanted:
            loads[name].wait()

    def every_peer(act):
        half = n_blk // 2
        act(lax.rem(blk + half, n_blk))

        def both(k, carry):
            act(lax.rem(blk + half + k, n_blk))
            act(lax.rem(blk + half - k, n_blk))
            return carry

        lax.fori_loop(1, half, both, 0)

    barrier = pltpu.get_barrier_semaphore()
    for d in (4, 5, 6, 7, 0, 1):
        pl.semaphore_signal(barrier, inc=1, device_id=step_to(d), device_id_type=MESH)
    every_peer(
        lambda peer: pl.semaphore_signal(
            barrier, inc=1, device_id=(face, peer), device_id_type=MESH
        )
    )

    sub = lax.broadcasted_iota(jnp.int32, TILE, 0)
    lane = lax.broadcasted_iota(jnp.int32, TILE, 1)
    x_pos, y_pos = lax.bitwise_and(sub, 3), lax.bitwise_and(lane, 3)
    first_x, last_x = x_pos == 0, x_pos == 3
    first_y, last_y = y_pos == 0, y_pos == 3
    sixth, five_sixths = F32(1.0 / 6.0), F32(5.0 / 6.0)
    gll_weight = jnp.where(first_x | last_x, sixth, five_sixths) * jnp.where(
        first_y | last_y, sixth, five_sixths
    )
    shifts = (-3, -2, -1, 1, 2, 3)

    loaded("cols", "weight", "tracer")
    surface = [
        jnp.broadcast_to(tracer_ref[0:1, 128 * h : 128 * h + 128], TILE) for h in range(16)
    ]
    for i in range(n_blk // 8):
        idx = cols_ref[8 * i : 8 * i + 8, :]
        weight = weight_ref[8 * i : 8 * i + 8, :]
        at = lane_gather(surface, lax.shift_right_logical(idx, 7), lax.bitwise_and(idx, 127))
        heat_pay[8 * i : 8 * i + 8, 0, :] = weight * at
        heat_pay[8 * i : 8 * i + 8, 1, :] = weight

    loaded("air", "wind", "jac")
    margin_pay[0] = air_ref[0:16, :]
    margin_pay[1] = wind_ref[0:16, :]
    margin_pay[2] = wind_ref[256:272, :]
    margin_pay[3] = jac_ref[...]
    for half in range(2):
        mass_ref[8 * half : 8 * half + 8, :] = gll_weight * jac_ref[8 * half : 8 * half + 8, :]

    loaded("send")
    for side in range(2):
        idx = jnp.broadcast_to(send_ref[side : side + 1, :], TILE)
        hi, lo = lax.shift_right_logical(idx, 7), lax.bitwise_and(idx, 127)
        for g in range(4):
            tiles = [tracer_ref[8 * g : 8 * g + 8, 128 * h : 128 * h + 128] for h in range(16)]
            rim_pay[side, 8 * g : 8 * g + 8, :] = lane_gather(tiles, hi, lo)

    taps_y = [(s, tap_table(y_pos, s)) for s in shifts]
    centre_y = tap_table(y_pos, 0)

    def slope_y(v):
        total = centre_y * v
        for s, tap in taps_y:
            total = total + tap * pltpu.roll(v, (-s) % 128, 1)
        return total

    def advance(field_at, target):
        def group(g, carry):
            half = lax.rem(g, 2) * 128
            planes = pl.ds(pl.multiple_of(g * 8, 8), 8)
            for e in range(4):
                fields = [field_at(g, 4 * e + k) for k in range(4)]
                for i in range(4):
                    x = 4 * e + i
                    slope_x = None
                    for k in range(4):
                        if DERIV[i][k]:
                            term = F32(DERIV[i][k]) * fields[k]
                            slope_x = term if slope_x is None else slope_x + term
                    wind_x = wind_ref[pl.ds(half + x, 8, stride=16), :]
                    wind_y = wind_ref[pl.ds(half + 256 + x, 8, stride=16), :]
                    tendency = wind_x * slope_x + wind_y * slope_y(fields[i])
                    moved = fields[i] - F32(TIME_STEP) * tendency
                    mass = jnp.broadcast_to(mass_ref[x : x + 1, :], TILE)
                    target[x + 1, planes, :] = mass * moved
            return carry

        lax.fori_loop(0, 6, group, 0)

    advance(lambda g, x: air_ref[pl.ds(g * 128 + x, 8, stride=16), :], weighted_1)
    loaded("rows", "land", "coef", "near", "vert", "area")
    build_hot(rows_ref, hot_rows)

    pl.semaphore_wait(barrier, n_blk - 1 + 6)

    def exchange(pay, inbox, slot):
        every_peer(
            lambda peer: pltpu.make_async_remote_copy(
                src_ref=pay.at[peer],
                dst_ref=inbox.at[blk],
                send_sem=all_send.at[slot],
                recv_sem=all_recv.at[slot],
                device_id=(face, peer),
                device_id_type=MESH,
            ).start()
        )

    def await_all(ref, sem):
        rest = ref.at[pl.ds(0, n_blk - 1)]
        pltpu.make_async_copy(rest, rest, sem).wait()

    started = []

    def send_near(src, dst, d, slot):
        copy = pltpu.make_async_remote_copy(
            src_ref=src,
            dst_ref=dst,
            send_sem=near_send.at[slot],
            recv_sem=near_recv.at[slot],
            device_id=step_to(d),
            device_id_type=MESH,
        )
        copy.start()
        started.append(copy)
        return copy

    exchange(heat_pay, heat_in, 0)
    heat_in[blk] = heat_pay[blk]

    margin_copies, surf_copies = [], []
    for d in range(8):
        low, high = MARGIN_ROWS[DIRECTIONS[d][0]]
        margin_copies.append(
            send_near(
                margin_pay.at[:, low:high, :],
                margin_in.at[REVERSE[d], :, 0 : high - low, :],
                d,
                d,
            )
        )

    rim_copies = [
        send_near(rim_pay.at[0], rim_in.at[1], 2, 24),
        send_near(rim_pay.at[1], rim_in.at[0], 3, 25),
    ]

    row_copies = [
        send_near(weighted_1.at[1], weighted_1.at[17], 0, 16),
        send_near(weighted_1.at[16], weighted_1.at[0], 1, 17),
    ]
    def ocean(first, last, tables=18):
        def block(j, carry):
            here = pl.ds(pl.multiple_of(j * 128, 128), 128)
            own = [tracer_ref[8 * g : 8 * g + 8, here] for g in range(4)]
            lateral = [jnp.zeros(TILE, F32) for g in range(4)]
            for e in range(6):
                idx = jnp.broadcast_to(near_ref[e : e + 1, here], TILE)
                coef = jnp.broadcast_to(coef_ref[e : e + 1, here], TILE)
                hi, lo = lax.shift_right_logical(idx, 7), lax.bitwise_and(idx, 127)
                found = [jnp.zeros(TILE, F32) for g in range(4)]
                for h in range(tables):
                    mine = hi == h
                    for g in range(4):
                        if h < 16:
                            tile = tracer_ref[8 * g : 8 * g + 8, 128 * h : 128 * h + 128]
                        else:
                            tile = rim_in[h - 16, 8 * g : 8 * g + 8, :]
                        found[g] = jnp.where(mine, jnp.take_along_axis(tile, lo, axis=1), found[g])
                for g in range(4):
                    lateral[g] = lateral[g] + coef * (found[g] - own[g])
            rate = jnp.broadcast_to(vert_ref[pl.ds(j, 1), :], TILE)
            for t in range(2):
                top, low = own[2 * t], own[2 * t + 1]
                down = [pltpu.roll(v, 1, 0) for v in (top, low)]
                up = [pltpu.roll(v, 7, 0) for v in (top, low)]
                above = [jnp.where(sub == 0, top, down[0]), jnp.where(sub == 0, down[0], down[1])]
                below = [jnp.where(sub == 7, up[1], up[0]), jnp.where(sub == 7, low, up[1])]
                for i, v in enumerate((top, low)):
                    g = 2 * t + i
                    vertical = rate * ((above[i] - v) + (below[i] - v))
                    ocean_out[8 * g : 8 * g + 8, here] = v + lateral[g] + vertical
            return carry

        lax.fori_loop(first, last, block, 0)

    def ocean_rim(first, last):
        def block(j, carry):
            here = pl.ds(pl.multiple_of(j * 128, 128), 128)
            lateral = [ocean_out[8 * g : 8 * g + 8, here] for g in range(4)]
            for e in range(6):
                idx = jnp.broadcast_to(near_ref[e : e + 1, here], TILE)
                coef = jnp.broadcast_to(coef_ref[e : e + 1, here], TILE)
                hi, lo = lax.shift_right_logical(idx, 7), lax.bitwise_and(idx, 127)
                for g in range(4):
                    found = jnp.zeros(TILE, F32)
                    for side in range(2):
                        tile = rim_in[side, 8 * g : 8 * g + 8, :]
                        found = jnp.where(
                            hi == 16 + side, jnp.take_along_axis(tile, lo, axis=1), found
                        )
                    lateral[g] = lateral[g] + coef * found
            for g in range(4):
                ocean_out[8 * g : 8 * g + 8, here] = lateral[g]
            return carry

        lax.fori_loop(first, last, block, 0)

    def sum_rows(weighted, column_pay):
        def group(g, carry):
            planes = pl.ds(pl.multiple_of(g * 8, 8), 8)
            packed = [jnp.zeros(TILE, F32), jnp.zeros(TILE, F32)]
            for x in range(16):
                total = weighted[x + 1, planes, :]
                if x % 4 == 0:
                    total = total + weighted[x, planes, :]
                if x % 4 == 3:
                    total = total + weighted[x + 2, planes, :]
                row_sum[x, planes, :] = total
                packed[0] = jnp.where(lane == x, pltpu.roll(total, x, 1), packed[0])
                packed[1] = jnp.where(lane == x, pltpu.roll(total, x + 1, 1), packed[1])
            for side in range(2):
                column_pay[side, planes, :] = packed[side]
            return carry

        lax.fori_loop(0, 6, group, 0)

    def sum_columns(column_in, store):
        def group(g, carry):
            planes = pl.ds(pl.multiple_of(g * 8, 8), 8)
            left, right = column_in[0, planes, :], column_in[1, planes, :]
            for x in range(16):
                v = row_sum[x, planes, :]
                before = jnp.where(
                    lane == 0, pltpu.roll(left, (128 - x) % 128, 1), pltpu.roll(v, 1, 1)
                )
                after = jnp.where(
                    lane == 127, pltpu.roll(right, 127 - x, 1), pltpu.roll(v, 127, 1)
                )
                total = v + jnp.where(first_y, before, 0.0) + jnp.where(last_y, after, 0.0)
                store(g, x, total * jnp.broadcast_to(inverse_ref[x : x + 1, :], TILE))
            return carry

        lax.fori_loop(0, 6, group, 0)

    build_hot(cols_ref, hot_cols)
    ocean(0, EARLY, 16)
    for copy in row_copies:
        copy.wait_recv()
    sum_rows(weighted_1, column_pay_1)
    column_copies = [
        send_near(column_pay_1.at[0], column_in_1.at[1], 2, 18),
        send_near(column_pay_1.at[1], column_in_1.at[0], 3, 19),
    ]

    for copy in margin_copies:
        copy.wait_recv()

    def widen(own, inbox):
        centre = [own[0:8], own[8:16], inbox(1)[0:8], inbox(0)[0:8]]
        right = [inbox(3)[0:8], inbox(3)[8:16], inbox(7)[0:8], inbox(5)[0:8]]
        left = [inbox(2)[0:8], inbox(2)[8:16], inbox(6)[0:8], inbox(4)[0:8]]
        return centre + [jnp.where(lane < 64, r, l) for r, l in zip(right, left)]

    def copy_sum(tiles):
        summed = []
        for side in range(2):
            part = tiles[4 * side : 4 * side + 4]
            prev = [pltpu.roll(v, 1, 0) for v in part]
            succ = [pltpu.roll(v, 7, 0) for v in part]
            for i in range(4):
                before = jnp.where(sub == 0, prev[i - 1], prev[i])
                after = jnp.where(sub == 7, succ[(i + 1) % 4], succ[i])
                summed.append(
                    part[i] + jnp.where(first_x, before, 0.0) + jnp.where(last_x, after, 0.0)
                )
        prev = [pltpu.roll(v, 1, 1) for v in summed]
        succ = [pltpu.roll(v, 127, 1) for v in summed]
        result = []
        for i in range(8):
            other = (i + 4) % 8
            before = jnp.where(lane == 0, prev[other], prev[i])
            after = jnp.where(lane == 127, succ[other], succ[i])
            result.append(
                summed[i] + jnp.where(first_y, before, 0.0) + jnp.where(last_y, after, 0.0)
            )
        return result

    taps_x = [(s, tap_table(x_pos, s)) for s in shifts]
    centre_x = tap_table(x_pos, 0)

    def without_surface(v, wind_x, wind_y):
        slope_x = centre_x * v
        for s, tap in taps_x:
            slope_x = slope_x + tap * pltpu.roll(v, (-s) % 8, 0)
        return v - F32(TIME_STEP) * (wind_x * slope_x + wind_y * slope_y(v)) - F32(RELAX) * v

    wide = [
        widen(margin_pay[q], lambda d, q=q: margin_in[d, q]) for q in range(4)
    ]
    wide_mass = [gll_weight * v for v in wide[3]]
    wide_inverse = [1.0 / v for v in copy_sum(wide_mass)]
    for i in range(8):
        base_ref[i] = without_surface(wide[0][i], wide[1][i], wide[2][i])
        wide_ref[0, i] = wide[1][i]
        wide_ref[1, i] = wide[2][i]
        wide_ref[2, i] = wide_mass[i]
        wide_ref[3, i] = wide_inverse[i]
    for half in range(2):
        inverse_ref[8 * half : 8 * half + 8, :] = wide_inverse[half]

    await_all(heat_in, all_recv.at[0])
    build_left(
        rows_ref,
        lambda base: (heat_in[pl.ds(base, 8), 0, :], heat_in[pl.ds(base, 8), 1, :]),
        left_ref,
    )
    heat, frac = scatter_sums(left_ref, hot_rows, 2)
    surf_pay[...] = (heat + land_ref[...] * air_ref[0:16, :]) / (frac + land_ref[...])
    for d in range(8):
        low, high = MARGIN_ROWS[DIRECTIONS[d][0]]
        surf_copies.append(
            send_near(
                surf_pay.at[low:high, :],
                surf_in.at[REVERSE[d], 0 : high - low, :],
                d,
                8 + d,
            )
        )

    for copy in column_copies:
        copy.wait_recv()

    def keep(g, x, v):
        field_1[x, pl.ds(pl.multiple_of(g * 8, 8), 8), :] = v

    sum_columns(column_in_1, keep)
    advance(lambda g, x: field_1[x, pl.ds(pl.multiple_of(g * 8, 8), 8), :], weighted_2)
    row_copies = [
        send_near(weighted_2.at[1], weighted_2.at[17], 0, 20),
        send_near(weighted_2.at[16], weighted_2.at[0], 1, 21),
    ]

    ocean(EARLY, EARLY + 1, 16)

    for copy in surf_copies:
        copy.wait_recv()
    surf = widen(surf_pay[...], lambda d: surf_in[d])
    moved = [
        wide_ref[2, i] * (base_ref[i] + F32(RELAX) * surf[i]) for i in range(8)
    ]
    field = [v * wide_ref[3, i] for i, v in enumerate(copy_sum(moved))]
    moved = [
        wide_ref[2, i]
        * (without_surface(field[i], wide_ref[0, i], wide_ref[1, i]) + F32(RELAX) * surf[i])
        for i in range(8)
    ]
    final = [v * wide_ref[3, i] for i, v in enumerate(copy_sum(moved)[0:2])]
    flux = [
        jnp.broadcast_to((final[h // 8] - surf[h // 8])[h % 8 : h % 8 + 1], TILE)
        for h in range(16)
    ]
    for i in range(n_blk // 8):
        idx = rows_ref[8 * i : 8 * i + 8, :]
        flux_pay[8 * i : 8 * i + 8, 0, :] = lane_gather(
            flux, lax.shift_right_logical(idx, 7), lax.bitwise_and(idx, 127)
        )
    exchange(flux_pay, flux_in, 1)
    flux_in[blk] = flux_pay[blk]

    for copy in rim_copies:
        copy.wait_recv()
    ocean(EARLY + 1, EARLY + 2)
    for copy in row_copies:
        copy.wait_recv()
    sum_rows(weighted_2, column_pay_2)
    column_copies = [
        send_near(column_pay_2.at[0], column_in_2.at[1], 2, 22),
        send_near(column_pay_2.at[1], column_in_2.at[0], 3, 23),
    ]
    ocean_rim(0, EARLY + 1)
    ocean(EARLY + 2, 13)
    for copy in column_copies:
        copy.wait_recv()

    def put_out(g, x, v):
        air_out[pl.ds(g * 128 + x, 8, stride=16), :] = v

    sum_columns(column_in_2, put_out)
    for half in range(2):
        air_out[8 * half : 8 * half + 8, :] = final[half]
    ocean(13, 16)

    await_all(flux_in, all_recv.at[1])
    build_left(
        cols_ref,
        lambda base: (weight_ref[pl.ds(base, 8), :] * flux_in[pl.ds(base, 8), 0, :],),
        left_out,
    )
    for copy in started:
        copy.wait_send()
    await_all(heat_pay, all_send.at[0])
    await_all(flux_pay, all_send.at[1])


def finish_kernel(air_ref, ocean_ref, left_ref, hot_ref, area_ref, air_out, ocean_out, top, sem):
    air_copy = pltpu.make_async_copy(air_ref, air_out, sem.at[0])
    ocean_copy = pltpu.make_async_copy(
        ocean_ref.at[pl.ds(8, 24), :], ocean_out.at[pl.ds(8, 24), :], sem.at[1]
    )
    air_copy.start()
    ocean_copy.start()
    (inflow,) = scatter_sums(left_ref, hot_ref, 1)
    gain = F32(FLUX_GAIN) * inflow / area_ref[...]
    first = lax.broadcasted_iota(jnp.int32, TILE, 0) == 0
    for h in range(16):
        here = slice(128 * h, 128 * h + 128)
        add = jnp.where(first, jnp.broadcast_to(gain[h : h + 1], TILE), 0.0)
        top[:, here] = ocean_ref[0:8, here] + add
    top_copy = pltpu.make_async_copy(top, ocean_out.at[pl.ds(0, 8), :], sem.at[2])
    top_copy.start()
    for copy in (air_copy, ocean_copy, top_copy):
        copy.wait()


def solution(mesh):
    n_face, n_blk = mesh.shape["face"], mesh.shape["blk"]

    def body(
        air_state,
        air_wind,
        jacobian,
        land_area,
        xgrid_rows,
        tracers,
        edge_coef,
        neighbours,
        vert_rate,
        ocean_area,
        send_list,
        xgrid_cols,
        xgrid_weights,
    ):
        air_shape, ocean_shape = air_state.shape, tracers.shape
        vmem = pltpu.VMEM
        air, ocean, left, hot, area = pl.pallas_call(
            lambda *refs: interval_kernel(n_face, n_blk, *refs),
            out_shape=(
                vmem((768, 128), F32),
                vmem((32, 2048), F32),
                vmem((16 * PARTS, 128 * n_blk), BF16),
                vmem((128, 128 * n_blk), BF16),
                vmem((16, 128), F32),
            ),
            in_specs=[pl.BlockSpec(memory_space=pl.ANY)] * 13,
            out_specs=(pl.BlockSpec(memory_space=vmem),) * 5,
            scratch_shapes=[
                vmem((768, 128), F32),
                vmem((512, 128), F32),
                vmem((16, 128), F32),
                vmem((16, 128), F32),
                vmem((n_blk, 128), jnp.int32),
                vmem((32, 2048), F32),
                vmem((6, 2048), F32),
                vmem((6, 2048), jnp.int32),
                vmem((16, 128), F32),
                vmem((2, 128), jnp.int32),
                vmem((n_blk, 128), jnp.int32),
                vmem((n_blk, 128), F32),
                pltpu.SemaphoreType.DMA((13,)),
                vmem((n_blk, 2, 128), F32),
                vmem((n_blk, 2, 128), F32),
                vmem((n_blk, 1, 128), F32),
                vmem((n_blk, 1, 128), F32),
                vmem((2, 32, 128), F32),
                vmem((2, 32, 128), F32),
                vmem((4, 16, 128), F32),
                vmem((8, 4, 16, 128), F32),
                vmem((16, 128), F32),
                vmem((8, 16, 128), F32),
                vmem((18, 48, 128), F32),
                vmem((18, 48, 128), F32),
                vmem((16, 48, 128), F32),
                vmem((2, 48, 128), F32),
                vmem((2, 48, 128), F32),
                vmem((2, 48, 128), F32),
                vmem((2, 48, 128), F32),
                vmem((16, 48, 128), F32),
                vmem((16, 128), F32),
                vmem((16, 128), F32),
                vmem((128, 128 * n_blk), BF16),
                vmem((32 * PARTS, 128 * n_blk), BF16),
                vmem((8, 8, 128), F32),
                vmem((4, 8, 8, 128), F32),
                pltpu.SemaphoreType.DMA((2,)),
                pltpu.SemaphoreType.DMA((2,)),
                pltpu.SemaphoreType.DMA((26,)),
                pltpu.SemaphoreType.DMA((26,)),
            ],
            compiler_params=pltpu.CompilerParams(collective_id=0, has_side_effects=True),
            name="interval",
        )(
            air_state.reshape(768, 128),
            air_wind.reshape(512, 128),
            jacobian,
            land_area,
            xgrid_rows[0],
            tracers.reshape(32, 2048),
            edge_coef,
            neighbours,
            vert_rate.reshape(16, 128),
            ocean_area.reshape(16, 128),
            send_list.reshape(2, 128),
            xgrid_cols[0],
            xgrid_weights[0],
        )
        air, ocean = pl.pallas_call(
            finish_kernel,
            out_shape=(
                jax.ShapeDtypeStruct((768, 128), F32),
                jax.ShapeDtypeStruct((32, 2048), F32),
            ),
            in_specs=[pl.BlockSpec(memory_space=vmem)] * 5,
            out_specs=(pl.BlockSpec(memory_space=pl.ANY),) * 2,
            scratch_shapes=[vmem((8, 2048), F32), pltpu.SemaphoreType.DMA((3,))],
            name="finish",
        )(*(pltpu.with_memory_space_constraint(v, vmem) for v in (air, ocean, left, hot, area)))
        return air.reshape(air_shape), ocean.reshape(ocean_shape)

    both = ("face", "blk")
    in_specs = (
        P(None, None, "face", "blk"),
        P(None, None, "face", "blk"),
        P("face", "blk"),
        P("face", "blk"),
        P(both, None, None),
        P(None, None, both),
        P(None, both),
        P(None, both),
        P(both),
        P(both),
        P(both, None),
        P(both, None, None),
        P(both, None, None),
    )
    out_specs = (P(None, None, "face", "blk"), P(None, None, both))
    return jax.shard_map(body, mesh=mesh, in_specs=in_specs, out_specs=out_specs, check_vma=False)
```
